512 devices in a mesh: rx: 32 (over x, z_lo), ry: 16 (over z_hi, y, core).
Axes of the slice: x: 4, y: 4, z: 16 (z_hi: 2, z_lo: 8; z = z_hi * 8 + z_lo), core: 2. Of those that a mesh axis runs over, the one named last changes fastest.
Arguments:
- cell_input: bfloat16 [128, 64, 64, 128], P('rx', 'ry'), may hold values from -6 to 6
- w_filter: bfloat16 [2, 32, 32], replicated, may hold values from -0.75 to 0.75
- w_gate: bfloat16 [2, 32, 32], replicated, may hold values from -0.75 to 0.75
- bias_filter: float32 [32], replicated, may hold values from -3 to 3
- bias_gate: float32 [32], replicated, may hold values from -3 to 3
- adjacency: bfloat16 [128, 64, 5, 4096], P('rx', 'ry'), may hold values from -0.3125 to 0.3125
- out_block: int32 [32, 16, 48], P('rx', 'ry'), may hold values from 0 to 15
- out_dev: int32 [32, 16, 48, 1], P('rx', 'ry'), may hold values from 0 to 31; in each aligned block of 48 rows (0 to 47, 48 to 95, ..., all dimensions but the last counted through in order) at most 2 rows name the same one
- out_target: int32 [32, 16, 48], P('rx', 'ry'), may hold values from 0 to 15
- out_tiles: bfloat16 [32, 16, 48, 4096], P('rx', 'ry'), may hold values from -0.75 to 0.75
- w_mix: bfloat16 [3, 32, 32], replicated, may hold values from -0.625 to 0.625
- bias_mix: float32 [32], replicated, may hold values from -3 to 3
Outputs:
- layer_output: bfloat16 [128, 64, 64, 128], P('rx', 'ry')
The draws below stay inside these ranges and needn't reach their ends.
Inputs may be any that keep to these rules, and one draw needn't show every extreme that they name: `out_dev`: among the 48 edges of one region no destination region row appears more than 2 times, and in some regions one appears exactly 2 times.
All inputs are finite; a program needn't handle non-finite values.
Results may differ from the reference program's by a relative error of at most 0.0045.
Values may be sent and summed in bfloat16 or wider, within the bound.
No kernel may reach another device: no remote copies, remote signals or barrier semaphores. Data moves between devices by JAX's collectives and lax.ppermute only.
A program may use at most 64 MiB of HBM per device.

```python
import math
import jax
import jax.numpy as jnp
import numpy as np
from jax import lax

C = 32
BSZ = 64
DILATION_STEP = 2
BR = 4
BC = 4
CAP = 2
E_DEV = 48
GR = 128
GC = 64
F = 128
TILE = 4096
N_RX = 32
N_RY = 16


def with_ends(array, own_key, low, high):
    dims = array.shape
    spot = [jax.random.randint(jax.random.fold_in(own_key, axis), (), 0, dims[axis]) for axis in range(len(dims))]
    array = array.at[tuple(spot)].set(low)
    longest = dims.index(max(dims))
    spot[longest] = (spot[longest] + 1) % dims[longest]
    return array.at[tuple(spot)].set(high)


def shard_levels(rng, dims, cuts, smallest, high):
    level = 1.0
    for dim, blocks in cuts:
        heights = jax.random.uniform(jax.random.fold_in(jax.random.fold_in(rng, 6), dim), (blocks,), jnp.float32, smallest / len(cuts), high / len(cuts))
        level = level * jnp.repeat(jnp.exp(heights), dims[dim] // blocks).reshape((-1,) + (1,) * (len(dims) - 1 - dim))
    return level


def routed_block(key, own, number, rows, amount, top, bound, skew):
    ranking = jax.random.permutation(key, amount)
    heavy_load, ordinary = portions_of(amount, rows * top, bound, skew, True), portions_of(amount, rows * top, bound, skew, False)
    places = jnp.arange(amount)

    def named(tallies, turn):
        used = int((tallies > 0).sum())
        fixed = max(1, used // 4)
        shifted = fixed + (places - fixed + turn * (used - fixed)) % max(1, amount - fixed)
        return jnp.zeros((amount,), jnp.int32).at[ranking[jnp.where(places < fixed, places, shifted)]].set(jnp.asarray(tallies, jnp.int32))

    tallies = jnp.where(number % 4 == 0, named(heavy_load, number // 4), named(ordinary, number - number // 4 - 1))
    mixed = jax.random.permutation(jax.random.fold_in(own, 3), amount)
    donor, receiver = mixed[0:amount // 2 * 2:2], mixed[1:amount // 2 * 2:2]
    margin = jnp.minimum(tallies[donor] - 1, bound - tallies[receiver]) // 2
    margin = jnp.where((donor == ranking[0]) | (receiver == ranking[0]) | (tallies[receiver] == 0), 0, jnp.maximum(margin, 0))
    shifted = jax.random.randint(jax.random.fold_in(own, 4), (amount // 2,), 0, 1 << 20) % (margin + 1)
    tallies = tallies.at[donor].add(-shifted).at[receiver].add(shifted)
    items = jnp.searchsorted(jnp.cumsum(tallies), jnp.arange(rows * top), side="right").astype(jnp.int32)
    table = items.reshape(top, rows).T
    table = table[jax.random.permutation(jax.random.fold_in(own, 1), rows)]
    turn = jax.random.randint(jax.random.fold_in(own, 2), (rows, 1), 0, top)
    return jnp.take_along_axis(table, (jnp.arange(top)[None, :] + turn) % top, axis=1)


def portions_of(count, total, limit, lean, full):
    weights = [(1 << 20) // math.isqrt(rank ** lean) + 1 for rank in range(1, count + 1)]
    largest = limit if full else min(limit, max(-(-total // count), total * weights[0] // sum(weights)))
    least = 1 if total - largest >= count - 1 else 0
    holding, rest = [largest] + [least] * (count - 1), total - largest - least * (count - 1)
    while rest > 0:
        free = [i for i in range(1, count) if holding[i] < largest] or [i for i in range(1, count) if holding[i] < limit]
        mass, budget = sum([weights[i] for i in free]), rest
        for i in free:
            more = min(limit - holding[i], max(1, budget * weights[i] // mass), rest)
            holding[i] = holding[i] + more
            rest = rest - more
    return np.array(holding)


def scatter_about(key, extent, deviation, limit, pieces=(), kind=jnp.bfloat16):
    entries = jax.random.normal(key, extent, jnp.float32) * deviation
    if len(pieces) > 0:
        entries = shard_levels(key, extent, pieces, -0.22, 0.18) * entries
    return jnp.clip(entries, min=-limit, max=limit).astype(kind)


def setup_inputs(seed: int = 0) -> dict:
    seeds = jax.random.split(jax.random.key(seed), 13)
    cell_input = scatter_about(seeds[0], (GR, GC, BSZ, F), 1.0, 6.0, ((0, 32), (1, 16)))
    w_filter = scatter_about(seeds[1], (2, C, C), (2 * C) ** -0.5, 0.75)
    w_gate = scatter_about(seeds[2], (2, C, C), (2 * C) ** -0.5, 0.75)
    bias_filter = scatter_about(seeds[3], (C,), 0.5, 3.0, (), jnp.float32)
    bias_gate = scatter_about(seeds[4], (C,), 0.5, 3.0, (), jnp.float32)
    adjacency = scatter_about(seeds[5], (GR, GC, 5, TILE), (5 * BSZ) ** -0.5, 0.3125, ((0, 32), (1, 16)))
    out_block = with_ends(jax.random.randint(seeds[6], (N_RX, N_RY, E_DEV), 0, BR * BC), jax.random.fold_in(seeds[6], 1), 0, (BR * BC) - 1).astype(jnp.int32)
    out_dev_keys = jax.random.split(jax.random.fold_in(seeds[7], 1), N_RX * N_RY * E_DEV // E_DEV)
    out_dev_turns = jax.random.permutation(jax.random.fold_in(seeds[7], 3), N_RX * N_RY * E_DEV // E_DEV)
    out_dev = jax.vmap(lambda own, number: routed_block(jax.random.fold_in(seeds[7], 2), own, number, E_DEV, N_RX, 1, CAP, 2))(out_dev_keys, out_dev_turns).reshape((N_RX, N_RY, E_DEV, 1))
    out_target = with_ends(jax.random.randint(seeds[8], (N_RX, N_RY, E_DEV), 0, BR * BC), jax.random.fold_in(seeds[8], 1), 0, (BR * BC) - 1).astype(jnp.int32)
    out_tiles = scatter_about(seeds[9], (N_RX, N_RY, E_DEV, TILE), BSZ ** -0.5, 0.75, ((0, 32), (1, 16)))
    w_mix = scatter_about(seeds[10], (3, C, C), (3 * C) ** -0.5, 0.625)
    bias_mix = scatter_about(seeds[11], (C,), 0.5, 3.0, (), jnp.float32)
    return {"cell_input": cell_input, "w_filter": w_filter, "w_gate": w_gate, "bias_filter": bias_filter, "bias_gate": bias_gate, "adjacency": adjacency, "out_block": out_block, "out_dev": out_dev, "out_target": out_target, "out_tiles": out_tiles, "w_mix": w_mix, "bias_mix": bias_mix}


def temporal_units(cell_row, w_filter, w_gate, bias_filter, bias_gate):
    channels = w_filter.shape[1]
    current_step = cell_row.astype(jnp.float32).reshape(cell_row.shape[0], cell_row.shape[1], -1, channels)
    earlier_step = jnp.concatenate([jnp.zeros_like(current_step[:, :, :DILATION_STEP]), current_step[:, :, :-DILATION_STEP]], axis=2)
    filter_taps = w_filter.astype(jnp.float32)
    gate_taps = w_gate.astype(jnp.float32)
    pre_filter = jnp.einsum("nbtc,cd->nbtd", current_step, filter_taps[1]) + jnp.einsum("nbtc,cd->nbtd", earlier_step, filter_taps[0]) + bias_filter
    pre_gate = jnp.einsum("nbtc,cd->nbtd", current_step, gate_taps[1]) + jnp.einsum("nbtc,cd->nbtd", earlier_step, gate_taps[0]) + bias_gate
    gated = jnp.tanh(pre_filter) * jax.nn.sigmoid(pre_gate)
    return gated.astype(jnp.bfloat16).reshape(cell_row.shape)


def far_term(signal, out_block, out_dev, out_target, out_tiles):
    far_sum = jnp.zeros(signal.shape, jnp.float32)

    def add_sender(far_sum, sender):
        strip_rows = lax.dynamic_slice_in_dim(signal, sender * BR, BR, 0)
        blocks = strip_rows.reshape(BR, N_RY, BC, BSZ, F).transpose(1, 0, 2, 3, 4).reshape(N_RY, BR * BC, BSZ, F)
        chosen = out_block[sender]
        source_feats = jax.vmap(lambda region, picks: region[picks])(blocks, chosen)
        edge_tiles = out_tiles[sender].astype(jnp.float32).reshape(N_RY, E_DEV, BSZ, BSZ)
        products = jnp.einsum("qeab,qebf->qeaf", edge_tiles, source_feats.astype(jnp.float32))
        targets = out_target[sender]
        dest_rows = out_dev[sender, :, :, 0] * BR + targets // BC
        dest_cols = jnp.arange(N_RY, dtype=jnp.int32)[:, None] * BC + targets % BC
        far_sum = far_sum.at[dest_rows, dest_cols].add(products)
        return far_sum, None

    far_sum, unused = lax.scan(add_sender, far_sum, jnp.arange(N_RX, dtype=jnp.int32))
    return far_sum


def stencil_row(block_row, padded, adjacency, far_sum):
    neighbours = (padded[block_row + 1, 1:-1], padded[block_row, 1:-1], padded[block_row + 2, 1:-1],
                  padded[block_row + 1, :-2], padded[block_row + 1, 2:])
    adj_row = adjacency[block_row].astype(jnp.float32).reshape(GC, 5, BSZ, BSZ)
    row_sum = far_sum[block_row]
    for offset in range(5):
        row_sum = row_sum + jnp.einsum("jab,jbf->jaf", adj_row[:, offset], neighbours[offset].astype(jnp.float32))
    return row_sum


def mix_row(gated_row, first_row, second_row, w_mix, bias_mix):
    shape_four = (gated_row.shape[0], gated_row.shape[1], -1, w_mix.shape[1])
    weights = w_mix.astype(jnp.float32)
    mixture = jnp.einsum("jatc,cd->jatd", gated_row.astype(jnp.float32).reshape(shape_four), weights[0])
    mixture = mixture + jnp.einsum("jatc,cd->jatd", first_row.astype(jnp.float32).reshape(shape_four), weights[1])
    mixture = mixture + jnp.einsum("jatc,cd->jatd", second_row.reshape(shape_four), weights[2], precision=lax.Precision.HIGHEST)
    mixture = mixture + bias_mix
    return mixture.reshape(gated_row.shape)


def reference(cell_input, w_filter, w_gate, bias_filter, bias_gate, adjacency, out_block, out_dev, out_target, out_tiles, w_mix, bias_mix):
    gated = lax.map(lambda cell_row: temporal_units(cell_row, w_filter, w_gate, bias_filter, bias_gate), cell_input)
    padding = ((1, 1), (1, 1), (0, 0), (0, 0))
    row_ids = jnp.arange(GR, dtype=jnp.int32)
    far_one = far_term(gated, out_block, out_dev, out_target, out_tiles)
    padded_one = jnp.pad(gated, padding)
    first_hop = lax.map(lambda block_row: stencil_row(block_row, padded_one, adjacency, far_one).astype(jnp.bfloat16), row_ids)
    far_two = far_term(first_hop, out_block, out_dev, out_target, out_tiles)
    padded_two = jnp.pad(first_hop, padding)

    def finish(block_row):
        second_row = stencil_row(block_row, padded_two, adjacency, far_two)
        mixture = mix_row(gated[block_row], first_hop[block_row], second_row, w_mix, bias_mix)
        return (cell_input[block_row].astype(jnp.float32) + mixture).astype(jnp.bfloat16)

    return lax.map(finish, row_ids)
```

```python
import jax
import jax.numpy as jnp
from jax import lax
from jax.sharding import PartitionSpec as P

DILATION_STEP = 2
CAP = 2


def group_eye(channels):
    group_members = 128 // channels
    input_signals = jnp.arange(group_members, dtype=jnp.int32)[:, None]
    output_signals = jnp.arange(group_members, dtype=jnp.int32)[None, :]
    return (input_signals, output_signals)


def time_tables(w_filter, w_gate, channels):
    group_members = 128 // channels
    input_signals, output_signals = group_eye(channels)
    diagonal = (input_signals == output_signals).astype(jnp.float32)
    within_group = (input_signals == output_signals - DILATION_STEP).astype(jnp.float32)
    across_groups = (input_signals == output_signals - DILATION_STEP + group_members).astype(
        jnp.float32
    )
    filter_taps = w_filter.astype(jnp.float32)
    gate_taps = w_gate.astype(jnp.float32)
    current_tab = jnp.concatenate(
        [
            jnp.kron(diagonal, filter_taps[1]) + jnp.kron(within_group, filter_taps[0]),
            jnp.kron(diagonal, gate_taps[1]) + jnp.kron(within_group, gate_taps[0]),
        ],
        axis=1,
    )
    earlier_tab = jnp.concatenate(
        [jnp.kron(across_groups, filter_taps[0]), jnp.kron(across_groups, gate_taps[0])], axis=1
    )
    return (current_tab.astype(jnp.bfloat16), earlier_tab.astype(jnp.bfloat16))


def gated_units(cell_input, current_tab, earlier_tab, bias_filter, bias_gate):
    block_rows, block_cols, block_size, features = cell_input.shape
    group_members = 128 // bias_filter.shape[0]
    grouped = cell_input.reshape(block_rows * block_cols * block_size, features // 128, 128)
    shifted = jnp.concatenate([jnp.zeros_like(grouped), grouped[:, :-1]], axis=1)
    pre_both = jnp.einsum("ngk,kj->ngj", grouped, current_tab, preferred_element_type=jnp.float32)
    pre_both = pre_both + jnp.einsum(
        "ngk,kj->ngj", shifted, earlier_tab, preferred_element_type=jnp.float32
    )
    filter_bias = jnp.tile(bias_filter, group_members)
    gate_bias = jnp.tile(bias_gate, group_members)
    gated = jnp.tanh(pre_both[..., :128] + filter_bias) * jax.nn.sigmoid(
        pre_both[..., 128:] + gate_bias
    )
    return gated.astype(jnp.bfloat16).reshape(cell_input.shape)


def shift_pairs(size, step):
    if step > 0:
        return [(i, i + 1) for i in range(size - 1)]
    return [(i + 1, i) for i in range(size - 1)]


def fetch_halo(signal):
    n_rx, n_ry = lax.axis_size("rx"), lax.axis_size("ry")
    above = lax.ppermute(signal[-1:], "rx", shift_pairs(n_rx, 1))
    below = lax.ppermute(signal[:1], "rx", shift_pairs(n_rx, -1))
    left = lax.ppermute(signal[:, -1:], "ry", shift_pairs(n_ry, 1))
    right = lax.ppermute(signal[:, :1], "ry", shift_pairs(n_ry, -1))
    return above, below, left, right


def local_terms(signal, tiles, halo):
    above, below, left, right = halo
    neighbours = (
        signal,
        jnp.concatenate([above, signal[:-1]], axis=0),
        jnp.concatenate([signal[1:], below], axis=0),
        jnp.concatenate([left, signal[:, :-1]], axis=1),
        jnp.concatenate([signal[:, 1:], right], axis=1),
    )
    stencil_sum = jnp.einsum(
        "ijab,ijbf->ijaf", tiles[:, :, 0], neighbours[0], preferred_element_type=jnp.float32
    )
    for offset in range(1, 5):
        stencil_sum = stencil_sum + jnp.einsum(
            "ijab,ijbf->ijaf",
            tiles[:, :, offset],
            neighbours[offset],
            preferred_element_type=jnp.float32,
        )
    return stencil_sum


def edge_select(out_dev, senders):
    destinations = out_dev.reshape(-1)
    owners = jnp.arange(senders, dtype=jnp.int32)
    dest_hits = (destinations[:, None] == owners[None, :]).astype(jnp.int32)
    edge_ranks = jnp.sum((jnp.cumsum(dest_hits, axis=0) - 1) * dest_hits, axis=1)
    slot_ids = jnp.arange(CAP, dtype=jnp.int32)
    select = dest_hits[:, :, None] * (edge_ranks[:, None, None] == slot_ids[None, None, :]).astype(
        jnp.int32
    )
    return select.reshape(select.shape[0], -1).astype(jnp.bfloat16)


def far_terms(recv_blocks, recv_tiles, recv_targets, nblocks):
    products = jnp.einsum(
        "sab,sbf->saf", recv_tiles, recv_blocks, preferred_element_type=jnp.float32
    )
    block_ids = jnp.arange(nblocks, dtype=jnp.float32)
    onehot = (recv_targets[None, :] == block_ids[:, None]).astype(jnp.float32)
    return jnp.einsum("ns,saf->naf", onehot, products, precision=lax.Precision.HIGHEST)


def local(
    cell_input,
    w_filter,
    w_gate,
    bias_filter,
    bias_gate,
    adjacency,
    out_block,
    out_dev,
    out_target,
    out_tiles,
    w_mix,
    bias_mix,
):
    channels = w_filter.shape[1]
    block_rows, block_cols, block_size, features = cell_input.shape
    nblocks = block_rows * block_cols
    n_rx = lax.axis_size("rx")
    tiles = adjacency.reshape(block_rows, block_cols, 5, block_size, block_size)
    current_tab, earlier_tab = time_tables(w_filter, w_gate, channels)
    gated = gated_units(cell_input, current_tab, earlier_tab, bias_filter, bias_gate)

    select = edge_select(out_dev, n_rx)
    sources = out_block.reshape(-1)
    edge_count = sources.shape[0]
    block_len = block_size * features
    tile_len = out_tiles.shape[-1]

    flat_gated = gated.reshape(nblocks, block_len)
    target_col = jnp.zeros((edge_count, 128), jnp.bfloat16).at[:, 0].set(
        (out_target.reshape(-1) + 1).astype(jnp.bfloat16)
    )
    payload = jnp.concatenate(
        [flat_gated[sources], out_tiles.reshape(edge_count, tile_len), target_col], axis=1
    )
    send_one = jnp.einsum(
        "es,ek->sk", select, payload, preferred_element_type=jnp.float32
    ).astype(jnp.bfloat16)
    send_one = send_one.reshape(n_rx, CAP, -1)
    halo_one = fetch_halo(gated)
    recv_one = lax.all_to_all(send_one, "rx", split_axis=0, concat_axis=0, tiled=True)
    recv_one = recv_one.reshape(n_rx * CAP, -1)
    recv_blocks = recv_one[:, :block_len].reshape(-1, block_size, features)
    recv_tiles = recv_one[:, block_len : block_len + tile_len].reshape(-1, block_size, block_size)
    recv_targets = recv_one[:, block_len + tile_len].astype(jnp.float32) - 1.0

    near_one = local_terms(gated, tiles, halo_one)
    far_one = far_terms(recv_blocks, recv_tiles, recv_targets, nblocks)
    first_hop = (near_one + far_one.reshape(gated.shape)).astype(jnp.bfloat16)

    flat_first = first_hop.reshape(nblocks, block_len)
    send_two = jnp.einsum(
        "es,ek->sk", select, flat_first[sources], preferred_element_type=jnp.float32
    ).astype(jnp.bfloat16)
    send_two = send_two.reshape(n_rx, CAP, block_size, features)
    halo_two = fetch_halo(first_hop)
    recv_two = lax.all_to_all(send_two, "rx", split_axis=0, concat_axis=0, tiled=True)
    recv_two = recv_two.reshape(n_rx * CAP, block_size, features)
    near_two = local_terms(first_hop, tiles, halo_two)
    far_two = far_terms(recv_two, recv_tiles, recv_targets, nblocks)
    second_hop = near_two + far_two.reshape(gated.shape)

    input_signals, output_signals = group_eye(channels)
    diagonal = (input_signals == output_signals).astype(jnp.float32)
    mix_weights = w_mix.astype(jnp.float32)
    table_zero = jnp.kron(diagonal, mix_weights[0]).astype(jnp.bfloat16)
    table_one = jnp.kron(diagonal, mix_weights[1]).astype(jnp.bfloat16)
    table_two = jnp.kron(diagonal, mix_weights[2])
    grouped_shape = (nblocks * block_size, features // 128, 128)
    mixture = jnp.einsum(
        "ngk,kj->ngj", gated.reshape(grouped_shape), table_zero, preferred_element_type=jnp.float32
    )
    mixture = mixture + jnp.einsum(
        "ngk,kj->ngj",
        first_hop.reshape(grouped_shape),
        table_one,
        preferred_element_type=jnp.float32,
    )
    mixture = mixture + jnp.einsum(
        "ngk,kj->ngj", second_hop.reshape(grouped_shape), table_two, precision=lax.Precision.HIGHEST
    )
    mixture = mixture + jnp.tile(bias_mix, 128 // channels)
    output_sum = cell_input.astype(jnp.float32) + mixture.reshape(cell_input.shape)
    return output_sum.astype(jnp.bfloat16)


def solution(mesh):
    in_specs = (
        P("rx", "ry", None, None),
        P(),
        P(),
        P(),
        P(),
        P("rx", "ry", None, None),
        P("rx", "ry", None),
        P("rx", "ry", None, None),
        P("rx", "ry", None),
        P("rx", "ry", None, None),
        P(),
        P(),
    )
    out_specs = P("rx", "ry", None, None)
    return jax.shard_map(local, mesh=mesh, in_specs=in_specs, out_specs=out_specs, check_vma=False)
```

```python
import jax
import jax.numpy as jnp
from jax import lax
from jax.sharding import PartitionSpec as P

DILATION_STEP = 2
CAP = 2


def group_eye(channels):
    group_members = 128 // channels
    input_signals = jnp.arange(group_members, dtype=jnp.int32)[:, None]
    output_signals = jnp.arange(group_members, dtype=jnp.int32)[None, :]
    return (input_signals, output_signals)


def time_tables(w_filter, w_gate, channels):
    group_members = 128 // channels
    input_signals, output_signals = group_eye(channels)
    diagonal = (input_signals == output_signals).astype(jnp.float32)
    within_group = (input_signals == output_signals - DILATION_STEP).astype(jnp.float32)
    across_groups = (input_signals == output_signals - DILATION_STEP + group_members).astype(
        jnp.float32
    )
    filter_taps = w_filter.astype(jnp.float32)
    gate_taps = w_gate.astype(jnp.float32)
    current_tab = jnp.concatenate(
        [
            jnp.kron(diagonal, filter_taps[1]) + jnp.kron(within_group, filter_taps[0]),
            jnp.kron(diagonal, gate_taps[1]) + jnp.kron(within_group, gate_taps[0]),
        ],
        axis=1,
    )
    earlier_tab = jnp.concatenate(
        [jnp.kron(across_groups, filter_taps[0]), jnp.kron(across_groups, gate_taps[0])], axis=1
    )
    return (current_tab.astype(jnp.bfloat16), earlier_tab.astype(jnp.bfloat16))


def gated_units(cell_input, current_tab, earlier_tab, bias_filter, bias_gate):
    block_rows, block_cols, block_size, features = cell_input.shape
    group_members = 128 // bias_filter.shape[0]
    grouped = cell_input.reshape(block_rows * block_cols * block_size, features // 128, 128)
    shifted = jnp.concatenate([jnp.zeros_like(grouped), grouped[:, :-1]], axis=1)
    pre_both = jnp.einsum("ngk,kj->ngj", grouped, current_tab, preferred_element_type=jnp.float32)
    pre_both = pre_both + jnp.einsum(
        "ngk,kj->ngj", shifted, earlier_tab, preferred_element_type=jnp.float32
    )
    filter_bias = jnp.tile(bias_filter, group_members)
    gate_bias = jnp.tile(bias_gate, group_members)
    gated = jnp.tanh(pre_both[..., :128] + filter_bias) * jax.nn.sigmoid(
        pre_both[..., 128:] + gate_bias
    )
    return gated.astype(jnp.bfloat16).reshape(cell_input.shape)


def shift_pairs(size, step):
    if step > 0:
        return [(i, i + 1) for i in range(size - 1)]
    return [(i + 1, i) for i in range(size - 1)]


def fetch_halo(signal):
    n_rx, n_ry = lax.axis_size("rx"), lax.axis_size("ry")
    above = lax.ppermute(signal[-1:], "rx", shift_pairs(n_rx, 1))
    below = lax.ppermute(signal[:1], "rx", shift_pairs(n_rx, -1))
    left = lax.ppermute(signal[:, -1:], "ry", shift_pairs(n_ry, 1))
    right = lax.ppermute(signal[:, :1], "ry", shift_pairs(n_ry, -1))
    return above, below, left, right


def local_terms(signal, tiles, halo):
    above, below, left, right = halo
    neighbours = (
        signal,
        jnp.concatenate([above, signal[:-1]], axis=0),
        jnp.concatenate([signal[1:], below], axis=0),
        jnp.concatenate([left, signal[:, :-1]], axis=1),
        jnp.concatenate([signal[:, 1:], right], axis=1),
    )
    stencil_sum = jnp.einsum(
        "ijab,ijbf->ijaf", tiles[:, :, 0], neighbours[0], preferred_element_type=jnp.float32
    )
    for offset in range(1, 5):
        stencil_sum = stencil_sum + jnp.einsum(
            "ijab,ijbf->ijaf",
            tiles[:, :, offset],
            neighbours[offset],
            preferred_element_type=jnp.float32,
        )
    return stencil_sum


def edge_select(out_dev, senders):
    destinations = out_dev.reshape(-1)
    owners = jnp.arange(senders, dtype=jnp.int32)
    dest_hits = (destinations[:, None] == owners[None, :]).astype(jnp.int32)
    edge_ranks = jnp.sum((jnp.cumsum(dest_hits, axis=0) - 1) * dest_hits, axis=1)
    slot_ids = jnp.arange(CAP, dtype=jnp.int32)
    select = dest_hits[:, :, None] * (edge_ranks[:, None, None] == slot_ids[None, None, :]).astype(
        jnp.int32
    )
    return select.reshape(select.shape[0], -1).astype(jnp.bfloat16)


def slot_targets(out_dev, out_target, cap):
    me = lax.axis_index("rx")
    info = jnp.stack([out_dev.reshape(-1), out_target.reshape(-1)], axis=0)
    every = lax.all_gather(info, "rx")
    hits = (every[:, 0] == me).astype(jnp.int32)
    ranks = jnp.cumsum(hits, axis=1) - 1
    slot_ids = jnp.arange(cap, dtype=jnp.int32)
    picks = hits[:, :, None] * (ranks[:, :, None] == slot_ids[None, None, :]).astype(jnp.int32)
    found = jnp.sum(picks * (every[:, 1, :, None] + 1), axis=1) - 1
    return found.reshape(-1)


def send_products(signal, edge_tiles, sources, select):
    block_rows, block_cols, block_size, features = signal.shape
    flat = signal.reshape(block_rows * block_cols, block_size, features)
    products = jnp.einsum(
        "eab,ebf->eaf", edge_tiles, flat[sources], preferred_element_type=jnp.float32
    ).astype(jnp.bfloat16)
    slots = jnp.einsum(
        "es,eaf->saf", select, products, preferred_element_type=jnp.float32
    ).astype(jnp.bfloat16)
    return slots.reshape(lax.axis_size("rx"), CAP, block_size, features)


def far_terms(received, targets, nblocks):
    received = received.reshape(targets.shape[0], -1)
    onehot = (targets[None, :] == jnp.arange(nblocks, dtype=jnp.int32)[:, None]).astype(
        jnp.bfloat16
    )
    return jnp.einsum("ns,sk->nk", onehot, received, preferred_element_type=jnp.float32)


def local(
    cell_input,
    w_filter,
    w_gate,
    bias_filter,
    bias_gate,
    adjacency,
    out_block,
    out_dev,
    out_target,
    out_tiles,
    w_mix,
    bias_mix,
):
    channels = w_filter.shape[1]
    block_rows, block_cols, block_size, features = cell_input.shape
    nblocks = block_rows * block_cols
    n_rx = lax.axis_size("rx")
    tiles = adjacency.reshape(block_rows, block_cols, 5, block_size, block_size)
    current_tab, earlier_tab = time_tables(w_filter, w_gate, channels)
    gated = gated_units(cell_input, current_tab, earlier_tab, bias_filter, bias_gate)

    select = edge_select(out_dev, n_rx)
    sources = out_block.reshape(-1)
    edge_tiles = out_tiles.reshape(-1, block_size, block_size)
    targets = slot_targets(out_dev, out_target, CAP)

    send_one = send_products(gated, edge_tiles, sources, select)
    halo_one = fetch_halo(gated)
    recv_one = lax.all_to_all(send_one, "rx", split_axis=0, concat_axis=0, tiled=True)
    near_one = local_terms(gated, tiles, halo_one)
    far_one = far_terms(recv_one, targets, nblocks)
    first_hop = (near_one + far_one.reshape(gated.shape)).astype(jnp.bfloat16)

    send_two = send_products(first_hop, edge_tiles, sources, select)
    halo_two = fetch_halo(first_hop)
    recv_two = lax.all_to_all(send_two, "rx", split_axis=0, concat_axis=0, tiled=True)
    near_two = local_terms(first_hop, tiles, halo_two)
    far_two = far_terms(recv_two, targets, nblocks)
    second_hop = near_two + far_two.reshape(gated.shape)

    input_signals, output_signals = group_eye(channels)
    diagonal = (input_signals == output_signals).astype(jnp.float32)
    mix_weights = w_mix.astype(jnp.float32)
    table_zero = jnp.kron(diagonal, mix_weights[0]).astype(jnp.bfloat16)
    table_one = jnp.kron(diagonal, mix_weights[1]).astype(jnp.bfloat16)
    table_two = jnp.kron(diagonal, mix_weights[2])
    grouped_shape = (nblocks * block_size, features // 128, 128)
    mixture = jnp.einsum(
        "ngk,kj->ngj", gated.reshape(grouped_shape), table_zero, preferred_element_type=jnp.float32
    )
    mixture = mixture + jnp.einsum(
        "ngk,kj->ngj",
        first_hop.reshape(grouped_shape),
        table_one,
        preferred_element_type=jnp.float32,
    )
    mixture = mixture + jnp.einsum(
        "ngk,kj->ngj", second_hop.reshape(grouped_shape), table_two, precision=lax.Precision.HIGHEST
    )
    mixture = mixture + jnp.tile(bias_mix, 128 // channels)
    output_sum = cell_input.astype(jnp.float32) + mixture.reshape(cell_input.shape)
    return output_sum.astype(jnp.bfloat16)


def solution(mesh):
    in_specs = (
        P("rx", "ry", None, None),
        P(),
        P(),
        P(),
        P(),
        P("rx", "ry", None, None),
        P("rx", "ry", None),
        P("rx", "ry", None, None),
        P("rx", "ry", None),
        P("rx", "ry", None, None),
        P(),
        P(),
    )
    out_specs = P("rx", "ry", None, None)
    return jax.shard_map(local, mesh=mesh, in_specs=in_specs, out_specs=out_specs, check_vma=False)
```

```python
import jax
import jax.numpy as jnp
from jax import lax
from jax.sharding import PartitionSpec as P

DILATION_STEP = 2
CAP = 2


def group_eye(channels):
    group_members = 128 // channels
    input_signals = jnp.arange(group_members, dtype=jnp.int32)[:, None]
    output_signals = jnp.arange(group_members, dtype=jnp.int32)[None, :]
    return (input_signals, output_signals)


def time_tables(w_filter, w_gate, channels):
    group_members = 128 // channels
    input_signals, output_signals = group_eye(channels)
    diagonal = (input_signals == output_signals).astype(jnp.float32)
    within_group = (input_signals == output_signals - DILATION_STEP).astype(jnp.float32)
    across_groups = (input_signals == output_signals - DILATION_STEP + group_members).astype(
        jnp.float32
    )
    filter_taps = w_filter.astype(jnp.float32)
    gate_taps = w_gate.astype(jnp.float32)
    current_tab = jnp.concatenate(
        [
            jnp.kron(diagonal, filter_taps[1]) + jnp.kron(within_group, filter_taps[0]),
            jnp.kron(diagonal, gate_taps[1]) + jnp.kron(within_group, gate_taps[0]),
        ],
        axis=1,
    )
    earlier_tab = jnp.concatenate(
        [jnp.kron(across_groups, filter_taps[0]), jnp.kron(across_groups, gate_taps[0])], axis=1
    )
    return (current_tab.astype(jnp.bfloat16), earlier_tab.astype(jnp.bfloat16))


def gated_units(cell_input, current_tab, earlier_tab, bias_filter, bias_gate):
    block_rows, block_cols, block_size, features = cell_input.shape
    group_members = 128 // bias_filter.shape[0]
    grouped = cell_input.reshape(block_rows * block_cols * block_size, features // 128, 128)
    shifted = jnp.concatenate([jnp.zeros_like(grouped), grouped[:, :-1]], axis=1)
    pre_both = jnp.einsum("ngk,kj->ngj", grouped, current_tab, preferred_element_type=jnp.float32)
    pre_both = pre_both + jnp.einsum(
        "ngk,kj->ngj", shifted, earlier_tab, preferred_element_type=jnp.float32
    )
    filter_bias = jnp.tile(bias_filter, group_members)
    gate_bias = jnp.tile(bias_gate, group_members)
    gated = jnp.tanh(pre_both[..., :128] + filter_bias) * jax.nn.sigmoid(
        pre_both[..., 128:] + gate_bias
    )
    return gated.astype(jnp.bfloat16).reshape(cell_input.shape)


def shift_pairs(size, step):
    if step > 0:
        return [(i, i + 1) for i in range(size - 1)]
    return [(i + 1, i) for i in range(size - 1)]


def fetch_halo(signal):
    n_rx, n_ry = lax.axis_size("rx"), lax.axis_size("ry")
    above = lax.ppermute(signal[-1:], "rx", shift_pairs(n_rx, 1))
    below = lax.ppermute(signal[:1], "rx", shift_pairs(n_rx, -1))
    left = lax.ppermute(signal[:, -1:], "ry", shift_pairs(n_ry, 1))
    right = lax.ppermute(signal[:, :1], "ry", shift_pairs(n_ry, -1))
    return above, below, left, right


def local_terms(signal, tiles, halo):
    above, below, left, right = halo
    neighbours = (
        signal,
        jnp.concatenate([above, signal[:-1]], axis=0),
        jnp.concatenate([signal[1:], below], axis=0),
        jnp.concatenate([left, signal[:, :-1]], axis=1),
        jnp.concatenate([signal[:, 1:], right], axis=1),
    )
    stencil_sum = jnp.einsum(
        "ijab,ijbf->ijaf", tiles[:, :, 0], neighbours[0], preferred_element_type=jnp.float32
    )
    for offset in range(1, 5):
        stencil_sum = stencil_sum + jnp.einsum(
            "ijab,ijbf->ijaf",
            tiles[:, :, offset],
            neighbours[offset],
            preferred_element_type=jnp.float32,
        )
    return stencil_sum


def edge_select(out_dev, senders):
    destinations = out_dev.reshape(-1)
    owners = jnp.arange(senders, dtype=jnp.int32)
    dest_hits = (destinations[:, None] == owners[None, :]).astype(jnp.int32)
    edge_ranks = jnp.sum((jnp.cumsum(dest_hits, axis=0) - 1) * dest_hits, axis=1)
    slot_ids = jnp.arange(CAP, dtype=jnp.int32)
    select = dest_hits[:, :, None] * (edge_ranks[:, None, None] == slot_ids[None, None, :]).astype(
        jnp.int32
    )
    return select.reshape(select.shape[0], -1).astype(jnp.bfloat16)


def slot_targets(select, out_target, n_rx):
    me = lax.axis_index("rx")
    mine = jnp.einsum(
        "es,e->s", select.astype(jnp.float32), (out_target.reshape(-1) + 1).astype(jnp.float32)
    ).reshape(n_rx, 1, CAP)
    owner = (jnp.arange(n_rx, dtype=jnp.int32) == me).astype(jnp.float32)
    table = mine * owner[None, :, None]
    found = lax.psum_scatter(table, "rx", scatter_dimension=0, tiled=True)
    return found.reshape(-1).astype(jnp.int32) - 1


def send_products(signal, edge_tiles, sources, select):
    block_rows, block_cols, block_size, features = signal.shape
    flat = signal.reshape(block_rows * block_cols, block_size, features)
    products = jnp.einsum(
        "eab,ebf->eaf", edge_tiles, flat[sources], preferred_element_type=jnp.float32
    ).astype(jnp.bfloat16)
    slots = jnp.einsum(
        "es,eaf->saf", select, products, preferred_element_type=jnp.float32
    ).astype(jnp.bfloat16)
    return slots.reshape(lax.axis_size("rx"), CAP, block_size, features)


def far_terms(received, targets, nblocks):
    received = received.reshape(targets.shape[0], -1)
    onehot = (targets[None, :] == jnp.arange(nblocks, dtype=jnp.int32)[:, None]).astype(
        jnp.bfloat16
    )
    return jnp.einsum("ns,sk->nk", onehot, received, preferred_element_type=jnp.float32)


def local(
    cell_input,
    w_filter,
    w_gate,
    bias_filter,
    bias_gate,
    adjacency,
    out_block,
    out_dev,
    out_target,
    out_tiles,
    w_mix,
    bias_mix,
):
    channels = w_filter.shape[1]
    block_rows, block_cols, block_size, features = cell_input.shape
    nblocks = block_rows * block_cols
    n_rx = lax.axis_size("rx")
    tiles = adjacency.reshape(block_rows, block_cols, 5, block_size, block_size)
    current_tab, earlier_tab = time_tables(w_filter, w_gate, channels)
    gated = gated_units(cell_input, current_tab, earlier_tab, bias_filter, bias_gate)

    select = edge_select(out_dev, n_rx)
    sources = out_block.reshape(-1)
    edge_tiles = out_tiles.reshape(-1, block_size, block_size)
    targets = slot_targets(select, out_target, n_rx)

    send_one = send_products(gated, edge_tiles, sources, select)
    halo_one = fetch_halo(gated)
    recv_one = lax.all_to_all(send_one, "rx", split_axis=0, concat_axis=0, tiled=True)
    near_one = local_terms(gated, tiles, halo_one)
    far_one = far_terms(recv_one, targets, nblocks)
    first_hop = (near_one + far_one.reshape(gated.shape)).astype(jnp.bfloat16)

    send_two = send_products(first_hop, edge_tiles, sources, select)
    halo_two = fetch_halo(first_hop)
    recv_two = lax.all_to_all(send_two, "rx", split_axis=0, concat_axis=0, tiled=True)
    near_two = local_terms(first_hop, tiles, halo_two)
    far_two = far_terms(recv_two, targets, nblocks)
    second_hop = near_two + far_two.reshape(gated.shape)

    input_signals, output_signals = group_eye(channels)
    diagonal = (input_signals == output_signals).astype(jnp.float32)
    mix_weights = w_mix.astype(jnp.float32)
    table_zero = jnp.kron(diagonal, mix_weights[0]).astype(jnp.bfloat16)
    table_one = jnp.kron(diagonal, mix_weights[1]).astype(jnp.bfloat16)
    table_two = jnp.kron(diagonal, mix_weights[2])
    grouped_shape = (nblocks * block_size, features // 128, 128)
    mixture = jnp.einsum(
        "ngk,kj->ngj", gated.reshape(grouped_shape), table_zero, preferred_element_type=jnp.float32
    )
    mixture = mixture + jnp.einsum(
        "ngk,kj->ngj",
        first_hop.reshape(grouped_shape),
        table_one,
        preferred_element_type=jnp.float32,
    )
    mixture = mixture + jnp.einsum(
        "ngk,kj->ngj", second_hop.reshape(grouped_shape), table_two, precision=lax.Precision.HIGHEST
    )
    mixture = mixture + jnp.tile(bias_mix, 128 // channels)
    output_sum = cell_input.astype(jnp.float32) + mixture.reshape(cell_input.shape)
    return output_sum.astype(jnp.bfloat16)


def solution(mesh):
    in_specs = (
        P("rx", "ry", None, None),
        P(),
        P(),
        P(),
        P(),
        P("rx", "ry", None, None),
        P("rx", "ry", None),
        P("rx", "ry", None, None),
        P("rx", "ry", None),
        P("rx", "ry", None, None),
        P(),
        P(),
    )
    out_specs = P("rx", "ry", None, None)
    return jax.shard_map(local, mesh=mesh, in_specs=in_specs, out_specs=out_specs, check_vma=False)
```

```python
import jax
import jax.numpy as jnp
from jax import lax
from jax.sharding import PartitionSpec as P

DILATION_STEP = 2
CAP = 2


def group_eye(channels):
    group_members = 128 // channels
    input_signals = jnp.arange(group_members, dtype=jnp.int32)[:, None]
    output_signals = jnp.arange(group_members, dtype=jnp.int32)[None, :]
    return (input_signals, output_signals)


def time_tables(w_filter, w_gate, channels):
    group_members = 128 // channels
    input_signals, output_signals = group_eye(channels)
    diagonal = (input_signals == output_signals).astype(jnp.float32)
    within_group = (input_signals == output_signals - DILATION_STEP).astype(jnp.float32)
    across_groups = (input_signals == output_signals - DILATION_STEP + group_members).astype(
        jnp.float32
    )
    filter_taps = w_filter.astype(jnp.float32)
    gate_taps = w_gate.astype(jnp.float32)
    current_tab = jnp.concatenate(
        [
            jnp.kron(diagonal, filter_taps[1]) + jnp.kron(within_group, filter_taps[0]),
            jnp.kron(diagonal, gate_taps[1]) + jnp.kron(within_group, gate_taps[0]),
        ],
        axis=1,
    )
    earlier_tab = jnp.concatenate(
        [jnp.kron(across_groups, filter_taps[0]), jnp.kron(across_groups, gate_taps[0])], axis=1
    )
    return (current_tab.astype(jnp.bfloat16), earlier_tab.astype(jnp.bfloat16))


def gated_units(cell_input, current_tab, earlier_tab, bias_filter, bias_gate):
    block_rows, block_cols, block_size, features = cell_input.shape
    group_members = 128 // bias_filter.shape[0]
    grouped = cell_input.reshape(block_rows * block_cols * block_size, features // 128, 128)
    shifted = jnp.concatenate([jnp.zeros_like(grouped), grouped[:, :-1]], axis=1)
    pre_both = jnp.einsum("ngk,kj->ngj", grouped, current_tab, preferred_element_type=jnp.float32)
    pre_both = pre_both + jnp.einsum(
        "ngk,kj->ngj", shifted, earlier_tab, preferred_element_type=jnp.float32
    )
    filter_bias = jnp.tile(bias_filter, group_members)
    gate_bias = jnp.tile(bias_gate, group_members)
    gated = jnp.tanh(pre_both[..., :128] + filter_bias) * jax.nn.sigmoid(
        pre_both[..., 128:] + gate_bias
    )
    return gated.astype(jnp.bfloat16).reshape(cell_input.shape)


def shift_pairs(size, step):
    if step > 0:
        return [(i, i + 1) for i in range(size - 1)]
    return [(i + 1, i) for i in range(size - 1)]


def fetch_halo(signal):
    n_rx, n_ry = lax.axis_size("rx"), lax.axis_size("ry")
    above = lax.ppermute(signal[-1:], "rx", shift_pairs(n_rx, 1))
    below = lax.ppermute(signal[:1], "rx", shift_pairs(n_rx, -1))
    left = lax.ppermute(signal[:, -1:], "ry", shift_pairs(n_ry, 1))
    right = lax.ppermute(signal[:, :1], "ry", shift_pairs(n_ry, -1))
    return above, below, left, right


def local_terms(signal, tiles, halo):
    above, below, left, right = halo
    neighbours = (
        signal,
        jnp.concatenate([above, signal[:-1]], axis=0),
        jnp.concatenate([signal[1:], below], axis=0),
        jnp.concatenate([left, signal[:, :-1]], axis=1),
        jnp.concatenate([signal[:, 1:], right], axis=1),
    )
    stencil_sum = jnp.einsum(
        "ijab,ijbf->ijaf", tiles[:, :, 0], neighbours[0], preferred_element_type=jnp.float32
    )
    for offset in range(1, 5):
        stencil_sum = stencil_sum + jnp.einsum(
            "ijab,ijbf->ijaf",
            tiles[:, :, offset],
            neighbours[offset],
            preferred_element_type=jnp.float32,
        )
    return stencil_sum


def edge_select(out_dev, senders):
    destinations = out_dev.reshape(-1)
    owners = jnp.arange(senders, dtype=jnp.int32)
    dest_hits = (destinations[:, None] == owners[None, :]).astype(jnp.int32)
    edge_ranks = jnp.sum((jnp.cumsum(dest_hits, axis=0) - 1) * dest_hits, axis=1)
    slot_ids = jnp.arange(CAP, dtype=jnp.int32)
    select = dest_hits[:, :, None] * (edge_ranks[:, None, None] == slot_ids[None, None, :]).astype(
        jnp.int32
    )
    return select.reshape(select.shape[0], -1).astype(jnp.bfloat16)


def slot_targets(select, out_target, n_rx):
    me = lax.axis_index("rx")
    mine = jnp.einsum(
        "es,e->s", select.astype(jnp.float32), (out_target.reshape(-1) + 1).astype(jnp.float32)
    ).reshape(n_rx, 1, CAP)
    owner = (jnp.arange(n_rx, dtype=jnp.int32) == me).astype(jnp.float32)
    table = mine * owner[None, :, None]
    found = lax.psum_scatter(table, "rx", scatter_dimension=0, tiled=True)
    return found.reshape(-1).astype(jnp.int32) - 1, jnp.sum(found) * 0.0


def send_products(signal, edge_tiles, sources, select, guard):
    block_rows, block_cols, block_size, features = signal.shape
    flat = signal.reshape(block_rows * block_cols, block_size, features)
    products = jnp.einsum(
        "eab,ebf->eaf", edge_tiles, flat[sources], preferred_element_type=jnp.float32
    ).astype(jnp.bfloat16)
    slots = jnp.einsum("es,eaf->saf", select, products, preferred_element_type=jnp.float32)
    slots = (slots + guard).astype(jnp.bfloat16)
    return slots.reshape(lax.axis_size("rx"), CAP, block_size, features)


def far_terms(received, targets, nblocks):
    received = received.reshape(targets.shape[0], -1)
    onehot = (targets[None, :] == jnp.arange(nblocks, dtype=jnp.int32)[:, None]).astype(
        jnp.bfloat16
    )
    return jnp.einsum("ns,sk->nk", onehot, received, preferred_element_type=jnp.float32)


def local(
    cell_input,
    w_filter,
    w_gate,
    bias_filter,
    bias_gate,
    adjacency,
    out_block,
    out_dev,
    out_target,
    out_tiles,
    w_mix,
    bias_mix,
):
    channels = w_filter.shape[1]
    block_rows, block_cols, block_size, features = cell_input.shape
    nblocks = block_rows * block_cols
    n_rx = lax.axis_size("rx")
    tiles = adjacency.reshape(block_rows, block_cols, 5, block_size, block_size)
    current_tab, earlier_tab = time_tables(w_filter, w_gate, channels)
    gated = gated_units(cell_input, current_tab, earlier_tab, bias_filter, bias_gate)

    select = edge_select(out_dev, n_rx)
    sources = out_block.reshape(-1)
    edge_tiles = out_tiles.reshape(-1, block_size, block_size)
    targets, guard = slot_targets(select, out_target, n_rx)

    send_one = send_products(gated, edge_tiles, sources, select, guard)
    halo_one = fetch_halo(gated)
    recv_one = lax.all_to_all(send_one, "rx", split_axis=0, concat_axis=0, tiled=True)
    near_one = local_terms(gated, tiles, halo_one)
    far_one = far_terms(recv_one, targets, nblocks)
    first_hop = (near_one + far_one.reshape(gated.shape)).astype(jnp.bfloat16)

    send_two = send_products(first_hop, edge_tiles, sources, select, 0.0)
    halo_two = fetch_halo(first_hop)
    recv_two = lax.all_to_all(send_two, "rx", split_axis=0, concat_axis=0, tiled=True)
    near_two = local_terms(first_hop, tiles, halo_two)
    far_two = far_terms(recv_two, targets, nblocks)
    second_hop = near_two + far_two.reshape(gated.shape)

    input_signals, output_signals = group_eye(channels)
    diagonal = (input_signals == output_signals).astype(jnp.float32)
    mix_weights = w_mix.astype(jnp.float32)
    table_zero = jnp.kron(diagonal, mix_weights[0]).astype(jnp.bfloat16)
    table_one = jnp.kron(diagonal, mix_weights[1]).astype(jnp.bfloat16)
    table_two = jnp.kron(diagonal, mix_weights[2])
    grouped_shape = (nblocks * block_size, features // 128, 128)
    mixture = jnp.einsum(
        "ngk,kj->ngj", gated.reshape(grouped_shape), table_zero, preferred_element_type=jnp.float32
    )
    mixture = mixture + jnp.einsum(
        "ngk,kj->ngj",
        first_hop.reshape(grouped_shape),
        table_one,
        preferred_element_type=jnp.float32,
    )
    mixture = mixture + jnp.einsum(
        "ngk,kj->ngj", second_hop.reshape(grouped_shape), table_two, precision=lax.Precision.HIGHEST
    )
    mixture = mixture + jnp.tile(bias_mix, 128 // channels)
    output_sum = cell_input.astype(jnp.float32) + mixture.reshape(cell_input.shape)
    return output_sum.astype(jnp.bfloat16)


def solution(mesh):
    in_specs = (
        P("rx", "ry", None, None),
        P(),
        P(),
        P(),
        P(),
        P("rx", "ry", None, None),
        P("rx", "ry", None),
        P("rx", "ry", None, None),
        P("rx", "ry", None),
        P("rx", "ry", None, None),
        P(),
        P(),
    )
    out_specs = P("rx", "ry", None, None)
    return jax.shard_map(local, mesh=mesh, in_specs=in_specs, out_specs=out_specs, check_vma=False)
```

```python
import jax
import jax.numpy as jnp
from jax import lax
from jax.sharding import PartitionSpec as P

DILATION_STEP = 2
CAP = 2


def group_eye(channels):
    group_members = 128 // channels
    input_signals = jnp.arange(group_members, dtype=jnp.int32)[:, None]
    output_signals = jnp.arange(group_members, dtype=jnp.int32)[None, :]
    return (input_signals, output_signals)


def time_tables(w_filter, w_gate, channels):
    group_members = 128 // channels
    input_signals, output_signals = group_eye(channels)
    diagonal = (input_signals == output_signals).astype(jnp.float32)
    within_group = (input_signals == output_signals - DILATION_STEP).astype(jnp.float32)
    across_groups = (input_signals == output_signals - DILATION_STEP + group_members).astype(
        jnp.float32
    )
    filter_taps = w_filter.astype(jnp.float32)
    gate_taps = w_gate.astype(jnp.float32)
    current_tab = jnp.concatenate(
        [
            jnp.kron(diagonal, filter_taps[1]) + jnp.kron(within_group, filter_taps[0]),
            jnp.kron(diagonal, gate_taps[1]) + jnp.kron(within_group, gate_taps[0]),
        ],
        axis=1,
    )
    earlier_tab = jnp.concatenate(
        [jnp.kron(across_groups, filter_taps[0]), jnp.kron(across_groups, gate_taps[0])], axis=1
    )
    return (current_tab.astype(jnp.bfloat16), earlier_tab.astype(jnp.bfloat16))


def gated_units(cell_input, current_tab, earlier_tab, bias_filter, bias_gate):
    block_rows, block_cols, block_size, features = cell_input.shape
    group_members = 128 // bias_filter.shape[0]
    grouped = cell_input.reshape(block_rows * block_cols * block_size, features // 128, 128)
    shifted = jnp.concatenate([jnp.zeros_like(grouped), grouped[:, :-1]], axis=1)
    pre_both = jnp.einsum("ngk,kj->ngj", grouped, current_tab, preferred_element_type=jnp.float32)
    pre_both = pre_both + jnp.einsum(
        "ngk,kj->ngj", shifted, earlier_tab, preferred_element_type=jnp.float32
    )
    filter_bias = jnp.tile(bias_filter, group_members)
    gate_bias = jnp.tile(bias_gate, group_members)
    gated = jnp.tanh(pre_both[..., :128] + filter_bias) * jax.nn.sigmoid(
        pre_both[..., 128:] + gate_bias
    )
    return gated.astype(jnp.bfloat16).reshape(cell_input.shape)


def shift_pairs(size, step):
    if step > 0:
        return [(i, i + 1) for i in range(size - 1)]
    return [(i + 1, i) for i in range(size - 1)]


def fetch_halo(signal):
    n_rx, n_ry = lax.axis_size("rx"), lax.axis_size("ry")
    above = lax.ppermute(signal[-1:], "rx", shift_pairs(n_rx, 1))
    below = lax.ppermute(signal[:1], "rx", shift_pairs(n_rx, -1))
    left = lax.ppermute(signal[:, -1:], "ry", shift_pairs(n_ry, 1))
    right = lax.ppermute(signal[:, :1], "ry", shift_pairs(n_ry, -1))
    return above, below, left, right


def local_terms(signal, tiles, halo):
    above, below, left, right = halo
    neighbours = (
        signal,
        jnp.concatenate([above, signal[:-1]], axis=0),
        jnp.concatenate([signal[1:], below], axis=0),
        jnp.concatenate([left, signal[:, :-1]], axis=1),
        jnp.concatenate([signal[:, 1:], right], axis=1),
    )
    stencil_sum = jnp.einsum(
        "ijab,ijbf->ijaf", tiles[:, :, 0], neighbours[0], preferred_element_type=jnp.float32
    )
    for offset in range(1, 5):
        stencil_sum = stencil_sum + jnp.einsum(
            "ijab,ijbf->ijaf",
            tiles[:, :, offset],
            neighbours[offset],
            preferred_element_type=jnp.float32,
        )
    return stencil_sum


def edge_select(out_dev, senders):
    destinations = out_dev.reshape(-1)
    owners = jnp.arange(senders, dtype=jnp.int32)
    dest_hits = (destinations[:, None] == owners[None, :]).astype(jnp.int32)
    edge_ranks = jnp.sum((jnp.cumsum(dest_hits, axis=0) - 1) * dest_hits, axis=1)
    slot_ids = jnp.arange(CAP, dtype=jnp.int32)
    select = dest_hits[:, :, None] * (edge_ranks[:, None, None] == slot_ids[None, None, :]).astype(
        jnp.int32
    )
    return select.reshape(select.shape[0], -1).astype(jnp.bfloat16)


def send_products(signal, edge_tiles, sources, select, target_col=None):
    block_rows, block_cols, block_size, features = signal.shape
    flat = signal.reshape(block_rows * block_cols, block_size, features)
    products = jnp.einsum(
        "eab,ebf->eaf", edge_tiles, flat[sources], preferred_element_type=jnp.float32
    ).astype(jnp.bfloat16)
    products = products.reshape(products.shape[0], -1)
    if target_col is not None:
        products = jnp.concatenate([products, target_col], axis=1)
    slots = jnp.einsum(
        "es,ek->sk", select, products, preferred_element_type=jnp.float32
    ).astype(jnp.bfloat16)
    return slots.reshape(lax.axis_size("rx"), CAP, -1)


def far_terms(received, targets, nblocks):
    received = received.reshape(targets.shape[0], -1)
    onehot = (targets[None, :] == jnp.arange(nblocks, dtype=jnp.int32)[:, None]).astype(
        jnp.bfloat16
    )
    return jnp.einsum("ns,sk->nk", onehot, received, preferred_element_type=jnp.float32)


def local(
    cell_input,
    w_filter,
    w_gate,
    bias_filter,
    bias_gate,
    adjacency,
    out_block,
    out_dev,
    out_target,
    out_tiles,
    w_mix,
    bias_mix,
):
    channels = w_filter.shape[1]
    block_rows, block_cols, block_size, features = cell_input.shape
    nblocks = block_rows * block_cols
    n_rx = lax.axis_size("rx")
    tiles = adjacency.reshape(block_rows, block_cols, 5, block_size, block_size)
    current_tab, earlier_tab = time_tables(w_filter, w_gate, channels)
    gated = gated_units(cell_input, current_tab, earlier_tab, bias_filter, bias_gate)

    select = edge_select(out_dev, n_rx)
    sources = out_block.reshape(-1)
    edge_tiles = out_tiles.reshape(-1, block_size, block_size)
    edge_count = sources.shape[0]
    block_len = block_size * features
    target_col = jnp.zeros((edge_count, 128), jnp.bfloat16).at[:, 0].set(
        (out_target.reshape(-1) + 1).astype(jnp.bfloat16)
    )

    send_one = send_products(gated, edge_tiles, sources, select, target_col)
    halo_one = fetch_halo(gated)
    recv_one = lax.all_to_all(send_one, "rx", split_axis=0, concat_axis=0, tiled=True)
    recv_one = recv_one.reshape(n_rx * CAP, -1)
    targets = recv_one[:, block_len].astype(jnp.int32) - 1
    recv_one = recv_one[:, :block_len]
    near_one = local_terms(gated, tiles, halo_one)
    far_one = far_terms(recv_one, targets, nblocks)
    first_hop = (near_one + far_one.reshape(gated.shape)).astype(jnp.bfloat16)

    send_two = send_products(first_hop, edge_tiles, sources, select)
    halo_two = fetch_halo(first_hop)
    recv_two = lax.all_to_all(send_two, "rx", split_axis=0, concat_axis=0, tiled=True)
    near_two = local_terms(first_hop, tiles, halo_two)
    far_two = far_terms(recv_two, targets, nblocks)
    second_hop = near_two + far_two.reshape(gated.shape)

    input_signals, output_signals = group_eye(channels)
    diagonal = (input_signals == output_signals).astype(jnp.float32)
    mix_weights = w_mix.astype(jnp.float32)
    table_zero = jnp.kron(diagonal, mix_weights[0]).astype(jnp.bfloat16)
    table_one = jnp.kron(diagonal, mix_weights[1]).astype(jnp.bfloat16)
    table_two = jnp.kron(diagonal, mix_weights[2])
    grouped_shape = (nblocks * block_size, features // 128, 128)
    mixture = jnp.einsum(
        "ngk,kj->ngj", gated.reshape(grouped_shape), table_zero, preferred_element_type=jnp.float32
    )
    mixture = mixture + jnp.einsum(
        "ngk,kj->ngj",
        first_hop.reshape(grouped_shape),
        table_one,
        preferred_element_type=jnp.float32,
    )
    mixture = mixture + jnp.einsum(
        "ngk,kj->ngj", second_hop.reshape(grouped_shape), table_two, precision=lax.Precision.HIGHEST
    )
    mixture = mixture + jnp.tile(bias_mix, 128 // channels)
    output_sum = cell_input.astype(jnp.float32) + mixture.reshape(cell_input.shape)
    return output_sum.astype(jnp.bfloat16)


def solution(mesh):
    in_specs = (
        P("rx", "ry", None, None),
        P(),
        P(),
        P(),
        P(),
        P("rx", "ry", None, None),
        P("rx", "ry", None),
        P("rx", "ry", None, None),
        P("rx", "ry", None),
        P("rx", "ry", None, None),
        P(),
        P(),
    )
    out_specs = P("rx", "ry", None, None)
    return jax.shard_map(local, mesh=mesh, in_specs=in_specs, out_specs=out_specs, check_vma=False)
```

```python
import jax
import jax.numpy as jnp
from jax import lax
from jax.experimental import pallas as pl
from jax.experimental.pallas import tpu as pltpu
from jax.sharding import PartitionSpec as P

DILATION_STEP = 2
CAP = 2


def group_eye(channels):
    group_members = 128 // channels
    input_signals = jnp.arange(group_members, dtype=jnp.int32)[:, None]
    output_signals = jnp.arange(group_members, dtype=jnp.int32)[None, :]
    return (input_signals, output_signals)


def time_tables(w_filter, w_gate, channels):
    group_members = 128 // channels
    input_signals, output_signals = group_eye(channels)
    diagonal = (input_signals == output_signals).astype(jnp.float32)
    within_group = (input_signals == output_signals - DILATION_STEP).astype(jnp.float32)
    across_groups = (input_signals == output_signals - DILATION_STEP + group_members).astype(
        jnp.float32
    )
    filter_taps = w_filter.astype(jnp.float32)
    gate_taps = w_gate.astype(jnp.float32)
    current_tab = jnp.concatenate(
        [
            jnp.kron(diagonal, filter_taps[1]) + jnp.kron(within_group, filter_taps[0]),
            jnp.kron(diagonal, gate_taps[1]) + jnp.kron(within_group, gate_taps[0]),
        ],
        axis=1,
    )
    earlier_tab = jnp.concatenate(
        [jnp.kron(across_groups, filter_taps[0]), jnp.kron(across_groups, gate_taps[0])], axis=1
    )
    return (current_tab.astype(jnp.bfloat16), earlier_tab.astype(jnp.bfloat16))


def gated_units(cell_input, current_tab, earlier_tab, bias_filter, bias_gate):
    block_rows, block_cols, block_size, features = cell_input.shape
    group_members = 128 // bias_filter.shape[0]
    grouped = cell_input.reshape(block_rows * block_cols * block_size, features // 128, 128)
    shifted = jnp.concatenate([jnp.zeros_like(grouped), grouped[:, :-1]], axis=1)
    pre_both = jnp.einsum("ngk,kj->ngj", grouped, current_tab, preferred_element_type=jnp.float32)
    pre_both = pre_both + jnp.einsum(
        "ngk,kj->ngj", shifted, earlier_tab, preferred_element_type=jnp.float32
    )
    filter_bias = jnp.tile(bias_filter, group_members)
    gate_bias = jnp.tile(bias_gate, group_members)
    gated = jnp.tanh(pre_both[..., :128] + filter_bias) * jax.nn.sigmoid(
        pre_both[..., 128:] + gate_bias
    )
    return gated.astype(jnp.bfloat16).reshape(cell_input.shape)


def shift_pairs(size, step):
    if step > 0:
        return [(i, i + 1) for i in range(size - 1)]
    return [(i + 1, i) for i in range(size - 1)]


def fetch_halo(signal):
    n_rx, n_ry = lax.axis_size("rx"), lax.axis_size("ry")
    above = lax.ppermute(signal[-1:], "rx", shift_pairs(n_rx, 1))
    below = lax.ppermute(signal[:1], "rx", shift_pairs(n_rx, -1))
    left = lax.ppermute(signal[:, -1:], "ry", shift_pairs(n_ry, 1))
    right = lax.ppermute(signal[:, :1], "ry", shift_pairs(n_ry, -1))
    return above, below, left, right


def local_terms(signal, tiles, halo):
    above, below, left, right = halo
    neighbours = (
        signal,
        jnp.concatenate([above, signal[:-1]], axis=0),
        jnp.concatenate([signal[1:], below], axis=0),
        jnp.concatenate([left, signal[:, :-1]], axis=1),
        jnp.concatenate([signal[:, 1:], right], axis=1),
    )
    stencil_sum = jnp.einsum(
        "ijab,ijbf->ijaf", tiles[:, :, 0], neighbours[0], preferred_element_type=jnp.float32
    )
    for offset in range(1, 5):
        stencil_sum = stencil_sum + jnp.einsum(
            "ijab,ijbf->ijaf",
            tiles[:, :, offset],
            neighbours[offset],
            preferred_element_type=jnp.float32,
        )
    return stencil_sum


def edge_select(out_dev, senders):
    destinations = out_dev.reshape(-1)
    owners = jnp.arange(senders, dtype=jnp.int32)
    dest_hits = (destinations[:, None] == owners[None, :]).astype(jnp.int32)
    edge_ranks = jnp.sum((jnp.cumsum(dest_hits, axis=0) - 1) * dest_hits, axis=1)
    slot_ids = jnp.arange(CAP, dtype=jnp.int32)
    select = dest_hits[:, :, None] * (edge_ranks[:, None, None] == slot_ids[None, None, :]).astype(
        jnp.int32
    )
    return select.reshape(select.shape[0], -1).astype(jnp.bfloat16)


def edge_slots(out_dev, senders):
    destinations = out_dev.reshape(-1)
    owners = jnp.arange(senders, dtype=jnp.int32)
    dest_hits = (destinations[:, None] == owners[None, :]).astype(jnp.int32)
    edge_ranks = jnp.sum((jnp.cumsum(dest_hits, axis=0) - 1) * dest_hits, axis=1)
    return destinations * CAP + edge_ranks


def product_kernel(src_ref, slot_ref, sig_ref, tile_ref, out_ref):
    out_ref[...] = jnp.zeros(out_ref.shape, out_ref.dtype)

    def body(edge, carry):
        block = sig_ref[src_ref[edge]]
        product = jnp.dot(tile_ref[edge], block, preferred_element_type=jnp.float32)
        out_ref[slot_ref[edge]] = product.astype(out_ref.dtype)
        return carry

    lax.fori_loop(0, tile_ref.shape[0], body, 0)


def send_products(signal, edge_tiles, sources, slots, select, target_col=None):
    block_rows, block_cols, block_size, features = signal.shape
    nblocks = block_rows * block_cols
    edge_count = edge_tiles.shape[0]
    nslots = lax.axis_size("rx") * CAP
    whole = lambda i, s, t: (0, 0, 0)
    products = pl.pallas_call(
        product_kernel,
        out_shape=jax.ShapeDtypeStruct((nslots, block_size, features), jnp.bfloat16),
        grid_spec=pltpu.PrefetchScalarGridSpec(
            num_scalar_prefetch=2,
            grid=(1,),
            in_specs=[
                pl.BlockSpec((nblocks, block_size, features), whole),
                pl.BlockSpec((edge_count, block_size, block_size), whole),
            ],
            out_specs=pl.BlockSpec((nslots, block_size, features), whole),
        ),
        cost_estimate=pl.CostEstimate(
            flops=2 * edge_count * block_size * block_size * features,
            bytes_accessed=2 * (nblocks + nslots) * block_size * features
            + 2 * edge_count * block_size * block_size,
            transcendentals=0,
        ),
    )(sources, slots, signal.reshape(nblocks, block_size, features), edge_tiles)
    if target_col is None:
        return products.reshape(lax.axis_size("rx"), CAP, block_size, features)
    slot_targets = jnp.einsum(
        "es,ek->sk", select, target_col, preferred_element_type=jnp.float32
    ).astype(jnp.bfloat16)
    payload = jnp.concatenate([products.reshape(nslots, -1), slot_targets], axis=1)
    return payload.reshape(lax.axis_size("rx"), CAP, -1)


def far_terms(received, targets, nblocks):
    received = received.reshape(targets.shape[0], -1)
    onehot = (targets[None, :] == jnp.arange(nblocks, dtype=jnp.int32)[:, None]).astype(
        jnp.bfloat16
    )
    return jnp.einsum("ns,sk->nk", onehot, received, preferred_element_type=jnp.float32)


def local(
    cell_input,
    w_filter,
    w_gate,
    bias_filter,
    bias_gate,
    adjacency,
    out_block,
    out_dev,
    out_target,
    out_tiles,
    w_mix,
    bias_mix,
):
    channels = w_filter.shape[1]
    block_rows, block_cols, block_size, features = cell_input.shape
    nblocks = block_rows * block_cols
    n_rx = lax.axis_size("rx")
    tiles = adjacency.reshape(block_rows, block_cols, 5, block_size, block_size)
    current_tab, earlier_tab = time_tables(w_filter, w_gate, channels)
    gated = gated_units(cell_input, current_tab, earlier_tab, bias_filter, bias_gate)

    select = edge_select(out_dev, n_rx)
    sources = out_block.reshape(-1)
    edge_tiles = out_tiles.reshape(-1, block_size, block_size)
    slots = edge_slots(out_dev, n_rx)
    edge_count = sources.shape[0]
    block_len = block_size * features
    target_col = jnp.zeros((edge_count, 128), jnp.bfloat16).at[:, 0].set(
        (out_target.reshape(-1) + 1).astype(jnp.bfloat16)
    )

    send_one = send_products(gated, edge_tiles, sources, slots, select, target_col)
    halo_one = fetch_halo(gated)
    recv_one = lax.all_to_all(send_one, "rx", split_axis=0, concat_axis=0, tiled=True)
    recv_one = recv_one.reshape(n_rx * CAP, -1)
    targets = recv_one[:, block_len].astype(jnp.int32) - 1
    recv_one = recv_one[:, :block_len]
    near_one = local_terms(gated, tiles, halo_one)
    far_one = far_terms(recv_one, targets, nblocks)
    first_hop = (near_one + far_one.reshape(gated.shape)).astype(jnp.bfloat16)

    send_two = send_products(first_hop, edge_tiles, sources, slots, select)
    halo_two = fetch_halo(first_hop)
    recv_two = lax.all_to_all(send_two, "rx", split_axis=0, concat_axis=0, tiled=True)
    near_two = local_terms(first_hop, tiles, halo_two)
    far_two = far_terms(recv_two, targets, nblocks)
    second_hop = near_two + far_two.reshape(gated.shape)

    input_signals, output_signals = group_eye(channels)
    diagonal = (input_signals == output_signals).astype(jnp.float32)
    mix_weights = w_mix.astype(jnp.float32)
    table_zero = jnp.kron(diagonal, mix_weights[0]).astype(jnp.bfloat16)
    table_one = jnp.kron(diagonal, mix_weights[1]).astype(jnp.bfloat16)
    table_two = jnp.kron(diagonal, mix_weights[2])
    grouped_shape = (nblocks * block_size, features // 128, 128)
    mixture = jnp.einsum(
        "ngk,kj->ngj", gated.reshape(grouped_shape), table_zero, preferred_element_type=jnp.float32
    )
    mixture = mixture + jnp.einsum(
        "ngk,kj->ngj",
        first_hop.reshape(grouped_shape),
        table_one,
        preferred_element_type=jnp.float32,
    )
    mixture = mixture + jnp.einsum(
        "ngk,kj->ngj", second_hop.reshape(grouped_shape), table_two, precision=lax.Precision.HIGHEST
    )
    mixture = mixture + jnp.tile(bias_mix, 128 // channels)
    output_sum = cell_input.astype(jnp.float32) + mixture.reshape(cell_input.shape)
    return output_sum.astype(jnp.bfloat16)


def solution(mesh):
    in_specs = (
        P("rx", "ry", None, None),
        P(),
        P(),
        P(),
        P(),
        P("rx", "ry", None, None),
        P("rx", "ry", None),
        P("rx", "ry", None, None),
        P("rx", "ry", None),
        P("rx", "ry", None, None),
        P(),
        P(),
    )
    out_specs = P("rx", "ry", None, None)
    return jax.shard_map(local, mesh=mesh, in_specs=in_specs, out_specs=out_specs, check_vma=False)
```

```python
import jax
import jax.numpy as jnp
from jax import lax
from jax.experimental import pallas as pl
from jax.experimental.pallas import tpu as pltpu
from jax.sharding import PartitionSpec as P

DILATION_STEP = 2
CAP = 2


def group_eye(channels):
    group_members = 128 // channels
    input_signals = jnp.arange(group_members, dtype=jnp.int32)[:, None]
    output_signals = jnp.arange(group_members, dtype=jnp.int32)[None, :]
    return (input_signals, output_signals)


def time_tables(w_filter, w_gate, channels):
    group_members = 128 // channels
    input_signals, output_signals = group_eye(channels)
    diagonal = (input_signals == output_signals).astype(jnp.float32)
    within_group = (input_signals == output_signals - DILATION_STEP).astype(jnp.float32)
    across_groups = (input_signals == output_signals - DILATION_STEP + group_members).astype(
        jnp.float32
    )
    filter_taps = w_filter.astype(jnp.float32)
    gate_taps = w_gate.astype(jnp.float32)
    current_tab = jnp.concatenate(
        [
            jnp.kron(diagonal, filter_taps[1]) + jnp.kron(within_group, filter_taps[0]),
            jnp.kron(diagonal, gate_taps[1]) + jnp.kron(within_group, gate_taps[0]),
        ],
        axis=1,
    )
    earlier_tab = jnp.concatenate(
        [jnp.kron(across_groups, filter_taps[0]), jnp.kron(across_groups, gate_taps[0])], axis=1
    )
    return (current_tab.astype(jnp.bfloat16), earlier_tab.astype(jnp.bfloat16))


def gated_units(cell_input, current_tab, earlier_tab, bias_filter, bias_gate):
    block_rows, block_cols, block_size, features = cell_input.shape
    group_members = 128 // bias_filter.shape[0]
    grouped = cell_input.reshape(block_rows * block_cols * block_size, features // 128, 128)
    shifted = jnp.concatenate([jnp.zeros_like(grouped), grouped[:, :-1]], axis=1)
    pre_both = jnp.einsum("ngk,kj->ngj", grouped, current_tab, preferred_element_type=jnp.float32)
    pre_both = pre_both + jnp.einsum(
        "ngk,kj->ngj", shifted, earlier_tab, preferred_element_type=jnp.float32
    )
    filter_bias = jnp.tile(bias_filter, group_members)
    gate_bias = jnp.tile(bias_gate, group_members)
    gated = jnp.tanh(pre_both[..., :128] + filter_bias) * jax.nn.sigmoid(
        pre_both[..., 128:] + gate_bias
    )
    return gated.astype(jnp.bfloat16).reshape(cell_input.shape)


def shift_pairs(size, step):
    if step > 0:
        return [(i, i + 1) for i in range(size - 1)]
    return [(i + 1, i) for i in range(size - 1)]


def fetch_halo(signal):
    n_rx, n_ry = lax.axis_size("rx"), lax.axis_size("ry")
    above = lax.ppermute(signal[-1:], "rx", shift_pairs(n_rx, 1))
    below = lax.ppermute(signal[:1], "rx", shift_pairs(n_rx, -1))
    left = lax.ppermute(signal[:, -1:], "ry", shift_pairs(n_ry, 1))
    right = lax.ppermute(signal[:, :1], "ry", shift_pairs(n_ry, -1))
    return above, below, left, right


def local_terms(signal, tiles, halo):
    above, below, left, right = halo
    neighbours = (
        signal,
        jnp.concatenate([above, signal[:-1]], axis=0),
        jnp.concatenate([signal[1:], below], axis=0),
        jnp.concatenate([left, signal[:, :-1]], axis=1),
        jnp.concatenate([signal[:, 1:], right], axis=1),
    )
    stencil_sum = jnp.einsum(
        "ijab,ijbf->ijaf", tiles[:, :, 0], neighbours[0], preferred_element_type=jnp.float32
    )
    for offset in range(1, 5):
        stencil_sum = stencil_sum + jnp.einsum(
            "ijab,ijbf->ijaf",
            tiles[:, :, offset],
            neighbours[offset],
            preferred_element_type=jnp.float32,
        )
    return stencil_sum


def edge_select(out_dev, senders):
    destinations = out_dev.reshape(-1)
    owners = jnp.arange(senders, dtype=jnp.int32)
    dest_hits = (destinations[:, None] == owners[None, :]).astype(jnp.int32)
    edge_ranks = jnp.sum((jnp.cumsum(dest_hits, axis=0) - 1) * dest_hits, axis=1)
    slot_ids = jnp.arange(CAP, dtype=jnp.int32)
    select = dest_hits[:, :, None] * (edge_ranks[:, None, None] == slot_ids[None, None, :]).astype(
        jnp.int32
    )
    return select.reshape(select.shape[0], -1).astype(jnp.bfloat16)


def edge_slots(out_dev, senders):
    destinations = out_dev.reshape(-1)
    owners = jnp.arange(senders, dtype=jnp.int32)
    dest_hits = (destinations[:, None] == owners[None, :]).astype(jnp.int32)
    edge_ranks = jnp.sum((jnp.cumsum(dest_hits, axis=0) - 1) * dest_hits, axis=1)
    return destinations * CAP + edge_ranks


def product_kernel(src_ref, slot_ref, sig_ref, tile_ref, out_ref):
    out_ref[...] = jnp.zeros(out_ref.shape, out_ref.dtype)

    def body(edge, carry):
        block = sig_ref[src_ref[edge]]
        product = jnp.dot(tile_ref[edge], block, preferred_element_type=jnp.float32)
        out_ref[slot_ref[edge]] = product.astype(out_ref.dtype)
        return carry

    lax.fori_loop(0, tile_ref.shape[0], body, 0, unroll=True)


def send_products(signal, edge_tiles, sources, slots, select, target_col=None):
    block_rows, block_cols, block_size, features = signal.shape
    nblocks = block_rows * block_cols
    edge_count = edge_tiles.shape[0]
    nslots = lax.axis_size("rx") * CAP
    whole = lambda i, s, t: (0, 0, 0)
    products = pl.pallas_call(
        product_kernel,
        out_shape=jax.ShapeDtypeStruct((nslots, block_size, features), jnp.bfloat16),
        grid_spec=pltpu.PrefetchScalarGridSpec(
            num_scalar_prefetch=2,
            grid=(1,),
            in_specs=[
                pl.BlockSpec((nblocks, block_size, features), whole),
                pl.BlockSpec((edge_count, block_size, block_size), whole),
            ],
            out_specs=pl.BlockSpec((nslots, block_size, features), whole),
        ),
        cost_estimate=pl.CostEstimate(
            flops=2 * edge_count * block_size * block_size * features,
            bytes_accessed=2 * (nblocks + nslots) * block_size * features
            + 2 * edge_count * block_size * block_size,
            transcendentals=0,
        ),
    )(sources, slots, signal.reshape(nblocks, block_size, features), edge_tiles)
    if target_col is None:
        return products.reshape(lax.axis_size("rx"), CAP, block_size, features)
    slot_targets = jnp.einsum(
        "es,ek->sk", select, target_col, preferred_element_type=jnp.float32
    ).astype(jnp.bfloat16)
    payload = jnp.concatenate([products.reshape(nslots, -1), slot_targets], axis=1)
    return payload.reshape(lax.axis_size("rx"), CAP, -1)


def far_terms(received, targets, nblocks):
    received = received.reshape(targets.shape[0], -1)
    onehot = (targets[None, :] == jnp.arange(nblocks, dtype=jnp.int32)[:, None]).astype(
        jnp.bfloat16
    )
    return jnp.einsum("ns,sk->nk", onehot, received, preferred_element_type=jnp.float32)


def local(
    cell_input,
    w_filter,
    w_gate,
    bias_filter,
    bias_gate,
    adjacency,
    out_block,
    out_dev,
    out_target,
    out_tiles,
    w_mix,
    bias_mix,
):
    channels = w_filter.shape[1]
    block_rows, block_cols, block_size, features = cell_input.shape
    nblocks = block_rows * block_cols
    n_rx = lax.axis_size("rx")
    tiles = adjacency.reshape(block_rows, block_cols, 5, block_size, block_size)
    current_tab, earlier_tab = time_tables(w_filter, w_gate, channels)
    gated = gated_units(cell_input, current_tab, earlier_tab, bias_filter, bias_gate)

    select = edge_select(out_dev, n_rx)
    sources = out_block.reshape(-1)
    edge_tiles = out_tiles.reshape(-1, block_size, block_size)
    slots = edge_slots(out_dev, n_rx)
    edge_count = sources.shape[0]
    block_len = block_size * features
    target_col = jnp.zeros((edge_count, 128), jnp.bfloat16).at[:, 0].set(
        (out_target.reshape(-1) + 1).astype(jnp.bfloat16)
    )

    send_one = send_products(gated, edge_tiles, sources, slots, select, target_col)
    halo_one = fetch_halo(gated)
    recv_one = lax.all_to_all(send_one, "rx", split_axis=0, concat_axis=0, tiled=True)
    recv_one = recv_one.reshape(n_rx * CAP, -1)
    targets = recv_one[:, block_len].astype(jnp.int32) - 1
    recv_one = recv_one[:, :block_len]
    near_one = local_terms(gated, tiles, halo_one)
    far_one = far_terms(recv_one, targets, nblocks)
    first_hop = (near_one + far_one.reshape(gated.shape)).astype(jnp.bfloat16)

    send_two = send_products(first_hop, edge_tiles, sources, slots, select)
    halo_two = fetch_halo(first_hop)
    recv_two = lax.all_to_all(send_two, "rx", split_axis=0, concat_axis=0, tiled=True)
    near_two = local_terms(first_hop, tiles, halo_two)
    far_two = far_terms(recv_two, targets, nblocks)
    second_hop = near_two + far_two.reshape(gated.shape)

    input_signals, output_signals = group_eye(channels)
    diagonal = (input_signals == output_signals).astype(jnp.float32)
    mix_weights = w_mix.astype(jnp.float32)
    table_zero = jnp.kron(diagonal, mix_weights[0]).astype(jnp.bfloat16)
    table_one = jnp.kron(diagonal, mix_weights[1]).astype(jnp.bfloat16)
    table_two = jnp.kron(diagonal, mix_weights[2])
    grouped_shape = (nblocks * block_size, features // 128, 128)
    mixture = jnp.einsum(
        "ngk,kj->ngj", gated.reshape(grouped_shape), table_zero, preferred_element_type=jnp.float32
    )
    mixture = mixture + jnp.einsum(
        "ngk,kj->ngj",
        first_hop.reshape(grouped_shape),
        table_one,
        preferred_element_type=jnp.float32,
    )
    mixture = mixture + jnp.einsum(
        "ngk,kj->ngj", second_hop.reshape(grouped_shape), table_two, precision=lax.Precision.HIGHEST
    )
    mixture = mixture + jnp.tile(bias_mix, 128 // channels)
    output_sum = cell_input.astype(jnp.float32) + mixture.reshape(cell_input.shape)
    return output_sum.astype(jnp.bfloat16)


def solution(mesh):
    in_specs = (
        P("rx", "ry", None, None),
        P(),
        P(),
        P(),
        P(),
        P("rx", "ry", None, None),
        P("rx", "ry", None),
        P("rx", "ry", None, None),
        P("rx", "ry", None),
        P("rx", "ry", None, None),
        P(),
        P(),
    )
    out_specs = P("rx", "ry", None, None)
    return jax.shard_map(local, mesh=mesh, in_specs=in_specs, out_specs=out_specs, check_vma=False)
```

```python
import jax
import jax.numpy as jnp
from jax import lax
from jax.experimental import pallas as pl
from jax.experimental.pallas import tpu as pltpu
from jax.sharding import PartitionSpec as P

DILATION_STEP = 2
CAP = 2


def group_eye(channels):
    group_members = 128 // channels
    input_signals = jnp.arange(group_members, dtype=jnp.int32)[:, None]
    output_signals = jnp.arange(group_members, dtype=jnp.int32)[None, :]
    return (input_signals, output_signals)


def time_tables(w_filter, w_gate, channels):
    group_members = 128 // channels
    input_signals, output_signals = group_eye(channels)
    diagonal = (input_signals == output_signals).astype(jnp.float32)
    within_group = (input_signals == output_signals - DILATION_STEP).astype(jnp.float32)
    across_groups = (input_signals == output_signals - DILATION_STEP + group_members).astype(
        jnp.float32
    )
    filter_taps = w_filter.astype(jnp.float32)
    gate_taps = w_gate.astype(jnp.float32)
    current_tab = jnp.concatenate(
        [
            jnp.kron(diagonal, filter_taps[1]) + jnp.kron(within_group, filter_taps[0]),
            jnp.kron(diagonal, gate_taps[1]) + jnp.kron(within_group, gate_taps[0]),
        ],
        axis=1,
    )
    earlier_tab = jnp.concatenate(
        [jnp.kron(across_groups, filter_taps[0]), jnp.kron(across_groups, gate_taps[0])], axis=1
    )
    return (current_tab.astype(jnp.bfloat16), earlier_tab.astype(jnp.bfloat16))


def gated_units(cell_input, current_tab, earlier_tab, bias_filter, bias_gate):
    block_rows, block_cols, block_size, features = cell_input.shape
    group_members = 128 // bias_filter.shape[0]
    grouped = cell_input.reshape(block_rows * block_cols * block_size, features // 128, 128)
    shifted = jnp.concatenate([jnp.zeros_like(grouped), grouped[:, :-1]], axis=1)
    pre_both = jnp.einsum("ngk,kj->ngj", grouped, current_tab, preferred_element_type=jnp.float32)
    pre_both = pre_both + jnp.einsum(
        "ngk,kj->ngj", shifted, earlier_tab, preferred_element_type=jnp.float32
    )
    filter_bias = jnp.tile(bias_filter, group_members)
    gate_bias = jnp.tile(bias_gate, group_members)
    gated = jnp.tanh(pre_both[..., :128] + filter_bias) * jax.nn.sigmoid(
        pre_both[..., 128:] + gate_bias
    )
    return gated.astype(jnp.bfloat16).reshape(cell_input.shape)


def shift_pairs(size, step):
    if step > 0:
        return [(i, i + 1) for i in range(size - 1)]
    return [(i + 1, i) for i in range(size - 1)]


def fetch_halo(signal):
    n_rx, n_ry = lax.axis_size("rx"), lax.axis_size("ry")
    above = lax.ppermute(signal[-1:], "rx", shift_pairs(n_rx, 1))
    below = lax.ppermute(signal[:1], "rx", shift_pairs(n_rx, -1))
    left = lax.ppermute(signal[:, -1:], "ry", shift_pairs(n_ry, 1))
    right = lax.ppermute(signal[:, :1], "ry", shift_pairs(n_ry, -1))
    return above, below, left, right


def local_terms(signal, tiles, halo):
    above, below, left, right = halo
    neighbours = (
        signal,
        jnp.concatenate([above, signal[:-1]], axis=0),
        jnp.concatenate([signal[1:], below], axis=0),
        jnp.concatenate([left, signal[:, :-1]], axis=1),
        jnp.concatenate([signal[:, 1:], right], axis=1),
    )
    stencil_sum = jnp.einsum(
        "ijab,ijbf->ijaf", tiles[:, :, 0], neighbours[0], preferred_element_type=jnp.float32
    )
    for offset in range(1, 5):
        stencil_sum = stencil_sum + jnp.einsum(
            "ijab,ijbf->ijaf",
            tiles[:, :, offset],
            neighbours[offset],
            preferred_element_type=jnp.float32,
        )
    return stencil_sum


def edge_select(out_dev, senders):
    destinations = out_dev.reshape(-1)
    owners = jnp.arange(senders, dtype=jnp.int32)
    dest_hits = (destinations[:, None] == owners[None, :]).astype(jnp.int32)
    edge_ranks = jnp.sum((jnp.cumsum(dest_hits, axis=0) - 1) * dest_hits, axis=1)
    slot_ids = jnp.arange(CAP, dtype=jnp.int32)
    select = dest_hits[:, :, None] * (edge_ranks[:, None, None] == slot_ids[None, None, :]).astype(
        jnp.int32
    )
    return select.reshape(select.shape[0], -1).astype(jnp.bfloat16)


def edge_slots(out_dev, senders):
    destinations = out_dev.reshape(-1)
    owners = jnp.arange(senders, dtype=jnp.int32)
    dest_hits = (destinations[:, None] == owners[None, :]).astype(jnp.int32)
    edge_ranks = jnp.sum((jnp.cumsum(dest_hits, axis=0) - 1) * dest_hits, axis=1)
    return destinations * CAP + edge_ranks


def product_kernel(src_ref, slot_ref, sig_ref, tile_ref, out_ref):
    out_ref[...] = jnp.zeros(out_ref.shape, out_ref.dtype)

    def body(edge, carry):
        block = sig_ref[src_ref[edge]]
        product = jnp.dot(tile_ref[edge], block, preferred_element_type=jnp.float32)
        out_ref[slot_ref[edge]] = product.astype(out_ref.dtype)
        return carry

    lax.fori_loop(0, tile_ref.shape[0], body, 0, unroll=True)


def send_products(signal, edge_tiles, sources, slots, select, target_col=None):
    block_rows, block_cols, block_size, features = signal.shape
    nblocks = block_rows * block_cols
    edge_count = edge_tiles.shape[0]
    nslots = lax.axis_size("rx") * CAP
    whole = lambda i, s, t: (0, 0, 0)
    products = pl.pallas_call(
        product_kernel,
        out_shape=jax.ShapeDtypeStruct((nslots, block_size, features), jnp.bfloat16),
        grid_spec=pltpu.PrefetchScalarGridSpec(
            num_scalar_prefetch=2,
            grid=(1,),
            in_specs=[
                pl.BlockSpec((nblocks, block_size, features), whole),
                pl.BlockSpec((edge_count, block_size, block_size), whole),
            ],
            out_specs=pl.BlockSpec((nslots, block_size, features), whole),
        ),
        cost_estimate=pl.CostEstimate(
            flops=2 * edge_count * block_size * block_size * features,
            bytes_accessed=2 * (nblocks + nslots) * block_size * features
            + 2 * edge_count * block_size * block_size,
            transcendentals=0,
        ),
    )(sources, slots, signal.reshape(nblocks, block_size, features), edge_tiles)
    if target_col is None:
        return products.reshape(lax.axis_size("rx"), CAP, block_size, features)
    slot_targets = jnp.einsum(
        "es,ek->sk", select, target_col, preferred_element_type=jnp.float32
    ).astype(jnp.bfloat16)
    payload = jnp.concatenate([products.reshape(nslots, -1), slot_targets], axis=1)
    return payload.reshape(lax.axis_size("rx"), CAP, -1)


def send_products_xla(signal, edge_tiles, sources, select, target_col):
    block_rows, block_cols, block_size, features = signal.shape
    flat = signal.reshape(block_rows * block_cols, block_size, features)
    products = jnp.einsum(
        "eab,ebf->eaf", edge_tiles, flat[sources], preferred_element_type=jnp.float32
    ).astype(jnp.bfloat16)
    products = jnp.concatenate([products.reshape(products.shape[0], -1), target_col], axis=1)
    slots = jnp.einsum(
        "es,ek->sk", select, products, preferred_element_type=jnp.float32
    ).astype(jnp.bfloat16)
    return slots.reshape(lax.axis_size("rx"), CAP, -1)


def far_terms(received, targets, nblocks):
    received = received.reshape(targets.shape[0], -1)
    onehot = (targets[None, :] == jnp.arange(nblocks, dtype=jnp.int32)[:, None]).astype(
        jnp.bfloat16
    )
    return jnp.einsum("ns,sk->nk", onehot, received, preferred_element_type=jnp.float32)


def local(
    cell_input,
    w_filter,
    w_gate,
    bias_filter,
    bias_gate,
    adjacency,
    out_block,
    out_dev,
    out_target,
    out_tiles,
    w_mix,
    bias_mix,
):
    channels = w_filter.shape[1]
    block_rows, block_cols, block_size, features = cell_input.shape
    nblocks = block_rows * block_cols
    n_rx = lax.axis_size("rx")
    tiles = adjacency.reshape(block_rows, block_cols, 5, block_size, block_size)
    current_tab, earlier_tab = time_tables(w_filter, w_gate, channels)
    gated = gated_units(cell_input, current_tab, earlier_tab, bias_filter, bias_gate)

    select = edge_select(out_dev, n_rx)
    sources = out_block.reshape(-1)
    edge_tiles = out_tiles.reshape(-1, block_size, block_size)
    slots = edge_slots(out_dev, n_rx)
    edge_count = sources.shape[0]
    block_len = block_size * features
    target_col = jnp.zeros((edge_count, 128), jnp.bfloat16).at[:, 0].set(
        (out_target.reshape(-1) + 1).astype(jnp.bfloat16)
    )

    send_one = send_products_xla(gated, edge_tiles, sources, select, target_col)
    halo_one = fetch_halo(gated)
    recv_one = lax.all_to_all(send_one, "rx", split_axis=0, concat_axis=0, tiled=True)
    recv_one = recv_one.reshape(n_rx * CAP, -1)
    targets = recv_one[:, block_len].astype(jnp.int32) - 1
    recv_one = recv_one[:, :block_len]
    near_one = local_terms(gated, tiles, halo_one)
    far_one = far_terms(recv_one, targets, nblocks)
    first_hop = (near_one + far_one.reshape(gated.shape)).astype(jnp.bfloat16)

    send_two = send_products(first_hop, edge_tiles, sources, slots, select)
    halo_two = fetch_halo(first_hop)
    recv_two = lax.all_to_all(send_two, "rx", split_axis=0, concat_axis=0, tiled=True)
    near_two = local_terms(first_hop, tiles, halo_two)
    far_two = far_terms(recv_two, targets, nblocks)
    second_hop = near_two + far_two.reshape(gated.shape)

    input_signals, output_signals = group_eye(channels)
    diagonal = (input_signals == output_signals).astype(jnp.float32)
    mix_weights = w_mix.astype(jnp.float32)
    table_zero = jnp.kron(diagonal, mix_weights[0]).astype(jnp.bfloat16)
    table_one = jnp.kron(diagonal, mix_weights[1]).astype(jnp.bfloat16)
    table_two = jnp.kron(diagonal, mix_weights[2])
    grouped_shape = (nblocks * block_size, features // 128, 128)
    mixture = jnp.einsum(
        "ngk,kj->ngj", gated.reshape(grouped_shape), table_zero, preferred_element_type=jnp.float32
    )
    mixture = mixture + jnp.einsum(
        "ngk,kj->ngj",
        first_hop.reshape(grouped_shape),
        table_one,
        preferred_element_type=jnp.float32,
    )
    mixture = mixture + jnp.einsum(
        "ngk,kj->ngj", second_hop.reshape(grouped_shape), table_two, precision=lax.Precision.HIGHEST
    )
    mixture = mixture + jnp.tile(bias_mix, 128 // channels)
    output_sum = cell_input.astype(jnp.float32) + mixture.reshape(cell_input.shape)
    return output_sum.astype(jnp.bfloat16)


def solution(mesh):
    in_specs = (
        P("rx", "ry", None, None),
        P(),
        P(),
        P(),
        P(),
        P("rx", "ry", None, None),
        P("rx", "ry", None),
        P("rx", "ry", None, None),
        P("rx", "ry", None),
        P("rx", "ry", None, None),
        P(),
        P(),
    )
    out_specs = P("rx", "ry", None, None)
    return jax.shard_map(local, mesh=mesh, in_specs=in_specs, out_specs=out_specs, check_vma=False)
```

```python
import jax
import jax.numpy as jnp
from jax import lax
from jax.experimental import pallas as pl
from jax.experimental.pallas import tpu as pltpu
from jax.sharding import PartitionSpec as P

DILATION_STEP = 2
CAP = 2


def group_eye(channels):
    group_members = 128 // channels
    input_signals = jnp.arange(group_members, dtype=jnp.int32)[:, None]
    output_signals = jnp.arange(group_members, dtype=jnp.int32)[None, :]
    return (input_signals, output_signals)


def time_tables(w_filter, w_gate, channels):
    group_members = 128 // channels
    input_signals, output_signals = group_eye(channels)
    diagonal = (input_signals == output_signals).astype(jnp.bfloat16)
    within_group = (input_signals == output_signals - DILATION_STEP).astype(jnp.bfloat16)
    across_groups = (input_signals == output_signals - DILATION_STEP + group_members).astype(
        jnp.bfloat16
    )
    current_tab = jnp.concatenate(
        [
            jnp.kron(diagonal, w_filter[1]) + jnp.kron(within_group, w_filter[0]),
            jnp.kron(diagonal, w_gate[1]) + jnp.kron(within_group, w_gate[0]),
        ],
        axis=1,
    )
    earlier_tab = jnp.concatenate(
        [jnp.kron(across_groups, w_filter[0]), jnp.kron(across_groups, w_gate[0])], axis=1
    )
    return (current_tab, earlier_tab)


def gated_units(cell_input, current_tab, earlier_tab, bias_filter, bias_gate):
    block_rows, block_cols, block_size, features = cell_input.shape
    group_members = 128 // bias_filter.shape[0]
    grouped = cell_input.reshape(block_rows * block_cols * block_size, features // 128, 128)
    shifted = jnp.concatenate([jnp.zeros_like(grouped), grouped[:, :-1]], axis=1)
    pre_both = jnp.einsum("ngk,kj->ngj", grouped, current_tab, preferred_element_type=jnp.float32)
    pre_both = pre_both + jnp.einsum(
        "ngk,kj->ngj", shifted, earlier_tab, preferred_element_type=jnp.float32
    )
    filter_bias = jnp.tile(bias_filter, group_members)
    gate_bias = jnp.tile(bias_gate, group_members)
    gated = jnp.tanh(pre_both[..., :128] + filter_bias) * jax.nn.sigmoid(
        pre_both[..., 128:] + gate_bias
    )
    return gated.astype(jnp.bfloat16).reshape(cell_input.shape)


def shift_pairs(size, step):
    if step > 0:
        return [(i, i + 1) for i in range(size - 1)]
    return [(i + 1, i) for i in range(size - 1)]


def fetch_halo(signal):
    n_rx, n_ry = lax.axis_size("rx"), lax.axis_size("ry")
    above = lax.ppermute(signal[-1:], "rx", shift_pairs(n_rx, 1))
    below = lax.ppermute(signal[:1], "rx", shift_pairs(n_rx, -1))
    left = lax.ppermute(signal[:, -1:], "ry", shift_pairs(n_ry, 1))
    right = lax.ppermute(signal[:, :1], "ry", shift_pairs(n_ry, -1))
    return above, below, left, right


def local_terms(signal, tiles, halo):
    above, below, left, right = halo
    neighbours = (
        signal,
        jnp.concatenate([above, signal[:-1]], axis=0),
        jnp.concatenate([signal[1:], below], axis=0),
        jnp.concatenate([left, signal[:, :-1]], axis=1),
        jnp.concatenate([signal[:, 1:], right], axis=1),
    )
    stencil_sum = jnp.einsum(
        "ijab,ijbf->ijaf", tiles[:, :, 0], neighbours[0], preferred_element_type=jnp.float32
    )
    for offset in range(1, 5):
        stencil_sum = stencil_sum + jnp.einsum(
            "ijab,ijbf->ijaf",
            tiles[:, :, offset],
            neighbours[offset],
            preferred_element_type=jnp.float32,
        )
    return stencil_sum


def edge_select(out_dev, senders):
    destinations = out_dev.reshape(-1)
    owners = jnp.arange(senders, dtype=jnp.int32)
    dest_hits = (destinations[:, None] == owners[None, :]).astype(jnp.int32)
    edge_ranks = jnp.sum((jnp.cumsum(dest_hits, axis=0) - 1) * dest_hits, axis=1)
    slot_ids = jnp.arange(CAP, dtype=jnp.int32)
    select = dest_hits[:, :, None] * (edge_ranks[:, None, None] == slot_ids[None, None, :]).astype(
        jnp.int32
    )
    return select.reshape(select.shape[0], -1).astype(jnp.bfloat16)


def edge_slots(out_dev, senders):
    destinations = out_dev.reshape(-1)
    owners = jnp.arange(senders, dtype=jnp.int32)
    dest_hits = (destinations[:, None] == owners[None, :]).astype(jnp.int32)
    edge_ranks = jnp.sum((jnp.cumsum(dest_hits, axis=0) - 1) * dest_hits, axis=1)
    return destinations * CAP + edge_ranks


def product_kernel(src_ref, slot_ref, sig_ref, tile_ref, out_ref):
    out_ref[...] = jnp.zeros(out_ref.shape, out_ref.dtype)

    def body(edge, carry):
        block = sig_ref[src_ref[edge]]
        product = jnp.dot(tile_ref[edge], block, preferred_element_type=jnp.float32)
        out_ref[slot_ref[edge]] = product.astype(out_ref.dtype)
        return carry

    lax.fori_loop(0, tile_ref.shape[0], body, 0, unroll=True)


def send_products(signal, edge_tiles, sources, slots, select, target_col=None):
    block_rows, block_cols, block_size, features = signal.shape
    nblocks = block_rows * block_cols
    edge_count = edge_tiles.shape[0]
    nslots = lax.axis_size("rx") * CAP
    whole = lambda i, s, t: (0, 0, 0)
    products = pl.pallas_call(
        product_kernel,
        out_shape=jax.ShapeDtypeStruct((nslots, block_size, features), jnp.bfloat16),
        grid_spec=pltpu.PrefetchScalarGridSpec(
            num_scalar_prefetch=2,
            grid=(1,),
            in_specs=[
                pl.BlockSpec((nblocks, block_size, features), whole),
                pl.BlockSpec((edge_count, block_size, block_size), whole),
            ],
            out_specs=pl.BlockSpec((nslots, block_size, features), whole),
        ),
        cost_estimate=pl.CostEstimate(
            flops=2 * edge_count * block_size * block_size * features,
            bytes_accessed=2 * (nblocks + nslots) * block_size * features
            + 2 * edge_count * block_size * block_size,
            transcendentals=0,
        ),
    )(sources, slots, signal.reshape(nblocks, block_size, features), edge_tiles)
    if target_col is None:
        return products.reshape(lax.axis_size("rx"), CAP, block_size, features)
    slot_targets = jnp.einsum(
        "es,ek->sk", select, target_col, preferred_element_type=jnp.float32
    ).astype(jnp.bfloat16)
    payload = jnp.concatenate([products.reshape(nslots, -1), slot_targets], axis=1)
    return payload.reshape(lax.axis_size("rx"), CAP, -1)


def send_products_xla(signal, edge_tiles, sources, select, target_col):
    block_rows, block_cols, block_size, features = signal.shape
    flat = signal.reshape(block_rows * block_cols, block_size, features)
    products = jnp.einsum(
        "eab,ebf->eaf", edge_tiles, flat[sources], preferred_element_type=jnp.float32
    ).astype(jnp.bfloat16)
    products = jnp.concatenate([products.reshape(products.shape[0], -1), target_col], axis=1)
    slots = jnp.einsum(
        "es,ek->sk", select, products, preferred_element_type=jnp.float32
    ).astype(jnp.bfloat16)
    return slots.reshape(lax.axis_size("rx"), CAP, -1)


def far_terms(received, targets, nblocks):
    senders, cap = received.shape[0], received.shape[1]
    received = received.reshape(senders, cap, -1)
    onehot = (targets[None] == jnp.arange(nblocks, dtype=jnp.int32)[:, None, None]).astype(
        jnp.bfloat16
    )
    return jnp.einsum("nrc,rck->nk", onehot, received, preferred_element_type=jnp.float32)


def local(
    cell_input,
    w_filter,
    w_gate,
    bias_filter,
    bias_gate,
    adjacency,
    out_block,
    out_dev,
    out_target,
    out_tiles,
    w_mix,
    bias_mix,
):
    channels = w_filter.shape[1]
    block_rows, block_cols, block_size, features = cell_input.shape
    nblocks = block_rows * block_cols
    n_rx = lax.axis_size("rx")
    tiles = adjacency.reshape(block_rows, block_cols, 5, block_size, block_size)
    current_tab, earlier_tab = time_tables(w_filter, w_gate, channels)
    gated = gated_units(cell_input, current_tab, earlier_tab, bias_filter, bias_gate)

    select = edge_select(out_dev, n_rx)
    sources = out_block.reshape(-1)
    edge_tiles = out_tiles.reshape(-1, block_size, block_size)
    slots = edge_slots(out_dev, n_rx)
    edge_count = sources.shape[0]
    block_len = block_size * features
    target_col = jnp.zeros((edge_count, 128), jnp.bfloat16).at[:, 0].set(
        (out_target.reshape(-1) + 1).astype(jnp.bfloat16)
    )

    send_one = send_products_xla(gated, edge_tiles, sources, select, target_col)
    halo_one = fetch_halo(gated)
    recv_one = lax.all_to_all(send_one, "rx", split_axis=0, concat_axis=0, tiled=True)
    targets = recv_one[:, :, block_len].astype(jnp.int32) - 1
    recv_one = recv_one[:, :, :block_len]
    near_one = local_terms(gated, tiles, halo_one)
    far_one = far_terms(recv_one, targets, nblocks)
    first_hop = (near_one + far_one.reshape(gated.shape)).astype(jnp.bfloat16)

    send_two = send_products(first_hop, edge_tiles, sources, slots, select)
    halo_two = fetch_halo(first_hop)
    recv_two = lax.all_to_all(send_two, "rx", split_axis=0, concat_axis=0, tiled=True)
    near_two = local_terms(first_hop, tiles, halo_two)
    far_two = far_terms(recv_two, targets, nblocks)
    second_hop = near_two + far_two.reshape(gated.shape)

    input_signals, output_signals = group_eye(channels)
    diagonal = (input_signals == output_signals).astype(jnp.float32)
    mix_weights = w_mix.astype(jnp.float32)
    table_zero = jnp.kron(diagonal.astype(jnp.bfloat16), w_mix[0])
    table_one = jnp.kron(diagonal.astype(jnp.bfloat16), w_mix[1])
    table_two = jnp.kron(diagonal, mix_weights[2])
    grouped_shape = (nblocks * block_size, features // 128, 128)
    mixture = jnp.einsum(
        "ngk,kj->ngj", gated.reshape(grouped_shape), table_zero, preferred_element_type=jnp.float32
    )
    mixture = mixture + jnp.einsum(
        "ngk,kj->ngj",
        first_hop.reshape(grouped_shape),
        table_one,
        preferred_element_type=jnp.float32,
    )
    mixture = mixture + jnp.einsum(
        "ngk,kj->ngj", second_hop.reshape(grouped_shape), table_two, precision=lax.Precision.HIGHEST
    )
    mixture = mixture + jnp.tile(bias_mix, 128 // channels)
    output_sum = cell_input.astype(jnp.float32) + mixture.reshape(cell_input.shape)
    return output_sum.astype(jnp.bfloat16)


def solution(mesh):
    in_specs = (
        P("rx", "ry", None, None),
        P(),
        P(),
        P(),
        P(),
        P("rx", "ry", None, None),
        P("rx", "ry", None),
        P("rx", "ry", None, None),
        P("rx", "ry", None),
        P("rx", "ry", None, None),
        P(),
        P(),
    )
    out_specs = P("rx", "ry", None, None)
    return jax.shard_map(local, mesh=mesh, in_specs=in_specs, out_specs=out_specs, check_vma=False)
```

```python
import jax
import jax.numpy as jnp
from jax import lax
from jax.experimental import pallas as pl
from jax.experimental.pallas import tpu as pltpu
from jax.sharding import PartitionSpec as P

DILATION_STEP = 2
CAP = 2


def group_eye(channels):
    group_members = 128 // channels
    input_signals = jnp.arange(group_members, dtype=jnp.int32)[:, None]
    output_signals = jnp.arange(group_members, dtype=jnp.int32)[None, :]
    return (input_signals, output_signals)


def time_tables(w_filter, w_gate, channels):
    group_members = 128 // channels
    input_signals, output_signals = group_eye(channels)
    diagonal = (input_signals == output_signals).astype(jnp.bfloat16)
    within_group = (input_signals == output_signals - DILATION_STEP).astype(jnp.bfloat16)
    across_groups = (input_signals == output_signals - DILATION_STEP + group_members).astype(
        jnp.bfloat16
    )
    current_tab = jnp.concatenate(
        [
            jnp.kron(diagonal, w_filter[1]) + jnp.kron(within_group, w_filter[0]),
            jnp.kron(diagonal, w_gate[1]) + jnp.kron(within_group, w_gate[0]),
        ],
        axis=1,
    )
    earlier_tab = jnp.concatenate(
        [jnp.kron(across_groups, w_filter[0]), jnp.kron(across_groups, w_gate[0])], axis=1
    )
    return (current_tab, earlier_tab)


def gated_units(cell_input, current_tab, earlier_tab, bias_filter, bias_gate):
    block_rows, block_cols, block_size, features = cell_input.shape
    group_members = 128 // bias_filter.shape[0]
    grouped = cell_input.reshape(block_rows * block_cols * block_size, features // 128, 128)
    shifted = jnp.concatenate([jnp.zeros_like(grouped), grouped[:, :-1]], axis=1)
    pre_both = jnp.einsum("ngk,kj->ngj", grouped, current_tab, preferred_element_type=jnp.float32)
    pre_both = pre_both + jnp.einsum(
        "ngk,kj->ngj", shifted, earlier_tab, preferred_element_type=jnp.float32
    )
    filter_bias = jnp.tile(bias_filter, group_members)
    gate_bias = jnp.tile(bias_gate, group_members)
    gated = jnp.tanh(pre_both[..., :128] + filter_bias) * jax.nn.sigmoid(
        pre_both[..., 128:] + gate_bias
    )
    return gated.astype(jnp.bfloat16).reshape(cell_input.shape)


def shift_pairs(size, step):
    if step > 0:
        return [(i, i + 1) for i in range(size - 1)]
    return [(i + 1, i) for i in range(size - 1)]


def fetch_halo(signal):
    n_rx, n_ry = lax.axis_size("rx"), lax.axis_size("ry")
    above = lax.ppermute(signal[-1:], "rx", shift_pairs(n_rx, 1))
    below = lax.ppermute(signal[:1], "rx", shift_pairs(n_rx, -1))
    left = lax.ppermute(signal[:, -1:], "ry", shift_pairs(n_ry, 1))
    right = lax.ppermute(signal[:, :1], "ry", shift_pairs(n_ry, -1))
    return above, below, left, right


def local_terms(signal, tiles, halo):
    above, below, left, right = halo
    neighbours = (
        signal,
        jnp.concatenate([above, signal[:-1]], axis=0),
        jnp.concatenate([signal[1:], below], axis=0),
        jnp.concatenate([left, signal[:, :-1]], axis=1),
        jnp.concatenate([signal[:, 1:], right], axis=1),
    )
    stencil_sum = jnp.einsum(
        "ijab,ijbf->ijaf", tiles[:, :, 0], neighbours[0], preferred_element_type=jnp.float32
    )
    for offset in range(1, 5):
        stencil_sum = stencil_sum + jnp.einsum(
            "ijab,ijbf->ijaf",
            tiles[:, :, offset],
            neighbours[offset],
            preferred_element_type=jnp.float32,
        )
    return stencil_sum


def edge_select(out_dev, senders):
    destinations = out_dev.reshape(-1)
    owners = jnp.arange(senders, dtype=jnp.int32)
    dest_hits = (destinations[:, None] == owners[None, :]).astype(jnp.int32)
    edge_ranks = jnp.sum((jnp.cumsum(dest_hits, axis=0) - 1) * dest_hits, axis=1)
    slot_ids = jnp.arange(CAP, dtype=jnp.int32)
    select = dest_hits[:, :, None] * (edge_ranks[:, None, None] == slot_ids[None, None, :]).astype(
        jnp.int32
    )
    return select.reshape(select.shape[0], -1).astype(jnp.bfloat16)


def edge_slots(out_dev, senders):
    destinations = out_dev.reshape(-1)
    owners = jnp.arange(senders, dtype=jnp.int32)
    dest_hits = (destinations[:, None] == owners[None, :]).astype(jnp.int32)
    edge_ranks = jnp.sum((jnp.cumsum(dest_hits, axis=0) - 1) * dest_hits, axis=1)
    return destinations * CAP + edge_ranks


def product_kernel(src_ref, slot_ref, sig_ref, tile_ref, out_ref):
    out_ref[...] = jnp.zeros(out_ref.shape, out_ref.dtype)

    def body(edge, carry):
        block = sig_ref[src_ref[edge]]
        product = jnp.dot(tile_ref[edge], block, preferred_element_type=jnp.float32)
        out_ref[slot_ref[edge]] = product.astype(out_ref.dtype)
        return carry

    lax.fori_loop(0, tile_ref.shape[0], body, 0, unroll=True)


def send_products(signal, edge_tiles, sources, slots, select, target_col=None):
    block_rows, block_cols, block_size, features = signal.shape
    nblocks = block_rows * block_cols
    edge_count = edge_tiles.shape[0]
    nslots = lax.axis_size("rx") * CAP
    whole = lambda i, s, t: (0, 0, 0)
    products = pl.pallas_call(
        product_kernel,
        out_shape=jax.ShapeDtypeStruct((nslots, block_size, features), jnp.bfloat16),
        grid_spec=pltpu.PrefetchScalarGridSpec(
            num_scalar_prefetch=2,
            grid=(1,),
            in_specs=[
                pl.BlockSpec((nblocks, block_size, features), whole),
                pl.BlockSpec((edge_count, block_size, block_size), whole),
            ],
            out_specs=pl.BlockSpec((nslots, block_size, features), whole),
        ),
        cost_estimate=pl.CostEstimate(
            flops=2 * edge_count * block_size * block_size * features,
            bytes_accessed=2 * (nblocks + nslots) * block_size * features
            + 2 * edge_count * block_size * block_size,
            transcendentals=0,
        ),
    )(sources, slots, signal.reshape(nblocks, block_size, features), edge_tiles)
    if target_col is None:
        return products.reshape(lax.axis_size("rx"), CAP, block_size, features)
    slot_targets = jnp.einsum(
        "es,ek->sk", select, target_col, preferred_element_type=jnp.float32
    ).astype(jnp.bfloat16)
    payload = jnp.concatenate([products.reshape(nslots, -1), slot_targets], axis=1)
    return payload.reshape(lax.axis_size("rx"), CAP, -1)


def send_products_xla(signal, edge_tiles, sources, select, target_col):
    block_rows, block_cols, block_size, features = signal.shape
    flat = signal.reshape(block_rows * block_cols, block_size, features)
    products = jnp.einsum(
        "eab,ebf->eaf", edge_tiles, flat[sources], preferred_element_type=jnp.float32
    ).astype(jnp.bfloat16)
    products = jnp.concatenate([products.reshape(products.shape[0], -1), target_col], axis=1)
    slots = jnp.einsum(
        "es,ek->sk", select, products, preferred_element_type=jnp.float32
    ).astype(jnp.bfloat16)
    return slots.reshape(lax.axis_size("rx"), CAP, -1)


def far_terms(received, targets, nblocks):
    onehot = (targets[None] == jnp.arange(nblocks, dtype=jnp.int32)[:, None, None]).astype(
        jnp.bfloat16
    )
    if received.ndim == 4:
        return jnp.einsum("nrc,rcaf->naf", onehot, received, preferred_element_type=jnp.float32)
    return jnp.einsum("nrc,rck->nk", onehot, received, preferred_element_type=jnp.float32)


def local(
    cell_input,
    w_filter,
    w_gate,
    bias_filter,
    bias_gate,
    adjacency,
    out_block,
    out_dev,
    out_target,
    out_tiles,
    w_mix,
    bias_mix,
):
    channels = w_filter.shape[1]
    block_rows, block_cols, block_size, features = cell_input.shape
    nblocks = block_rows * block_cols
    n_rx = lax.axis_size("rx")
    tiles = adjacency.reshape(block_rows, block_cols, 5, block_size, block_size)
    current_tab, earlier_tab = time_tables(w_filter, w_gate, channels)
    gated = gated_units(cell_input, current_tab, earlier_tab, bias_filter, bias_gate)

    select = edge_select(out_dev, n_rx)
    sources = out_block.reshape(-1)
    edge_tiles = out_tiles.reshape(-1, block_size, block_size)
    slots = edge_slots(out_dev, n_rx)
    edge_count = sources.shape[0]
    block_len = block_size * features
    target_col = jnp.zeros((edge_count, 128), jnp.bfloat16).at[:, 0].set(
        (out_target.reshape(-1) + 1).astype(jnp.bfloat16)
    )

    send_one = send_products_xla(gated, edge_tiles, sources, select, target_col)
    halo_one = fetch_halo(gated)
    recv_one = lax.all_to_all(send_one, "rx", split_axis=0, concat_axis=0, tiled=True)
    targets = recv_one[:, :, block_len].astype(jnp.int32) - 1
    near_one = local_terms(gated, tiles, halo_one)
    far_one = far_terms(recv_one, targets, nblocks)[:, :block_len]
    first_hop = (near_one + far_one.reshape(gated.shape)).astype(jnp.bfloat16)

    send_two = send_products(first_hop, edge_tiles, sources, slots, select)
    halo_two = fetch_halo(first_hop)
    recv_two = lax.all_to_all(send_two, "rx", split_axis=0, concat_axis=0, tiled=True)
    near_two = local_terms(first_hop, tiles, halo_two)
    far_two = far_terms(recv_two, targets, nblocks)
    second_hop = near_two + far_two.reshape(gated.shape)

    input_signals, output_signals = group_eye(channels)
    diagonal = (input_signals == output_signals).astype(jnp.float32)
    mix_weights = w_mix.astype(jnp.float32)
    table_zero = jnp.kron(diagonal.astype(jnp.bfloat16), w_mix[0])
    table_one = jnp.kron(diagonal.astype(jnp.bfloat16), w_mix[1])
    table_two = jnp.kron(diagonal, mix_weights[2])
    grouped_shape = (nblocks * block_size, features // 128, 128)
    mixture = jnp.einsum(
        "ngk,kj->ngj", gated.reshape(grouped_shape), table_zero, preferred_element_type=jnp.float32
    )
    mixture = mixture + jnp.einsum(
        "ngk,kj->ngj",
        first_hop.reshape(grouped_shape),
        table_one,
        preferred_element_type=jnp.float32,
    )
    mixture = mixture + jnp.einsum(
        "ngk,kj->ngj", second_hop.reshape(grouped_shape), table_two, precision=lax.Precision.HIGHEST
    )
    mixture = mixture + jnp.tile(bias_mix, 128 // channels)
    output_sum = cell_input.astype(jnp.float32) + mixture.reshape(cell_input.shape)
    return output_sum.astype(jnp.bfloat16)


def solution(mesh):
    in_specs = (
        P("rx", "ry", None, None),
        P(),
        P(),
        P(),
        P(),
        P("rx", "ry", None, None),
        P("rx", "ry", None),
        P("rx", "ry", None, None),
        P("rx", "ry", None),
        P("rx", "ry", None, None),
        P(),
        P(),
    )
    out_specs = P("rx", "ry", None, None)
    return jax.shard_map(local, mesh=mesh, in_specs=in_specs, out_specs=out_specs, check_vma=False)
```

```python
import jax
import jax.numpy as jnp
from jax import lax
from jax.experimental import pallas as pl
from jax.experimental.pallas import tpu as pltpu
from jax.sharding import PartitionSpec as P

DILATION_STEP = 2
CAP = 2


def group_eye(channels):
    group_members = 128 // channels
    input_signals = jnp.arange(group_members, dtype=jnp.int32)[:, None]
    output_signals = jnp.arange(group_members, dtype=jnp.int32)[None, :]
    return (input_signals, output_signals)


def time_tables(w_filter, w_gate, channels):
    group_members = 128 // channels
    input_signals, output_signals = group_eye(channels)
    diagonal = (input_signals == output_signals).astype(jnp.bfloat16)
    within_group = (input_signals == output_signals - DILATION_STEP).astype(jnp.bfloat16)
    across_groups = (input_signals == output_signals - DILATION_STEP + group_members).astype(
        jnp.bfloat16
    )
    current_tab = jnp.concatenate(
        [
            jnp.kron(diagonal, w_filter[1]) + jnp.kron(within_group, w_filter[0]),
            jnp.kron(diagonal, w_gate[1]) + jnp.kron(within_group, w_gate[0]),
        ],
        axis=1,
    )
    earlier_tab = jnp.concatenate(
        [jnp.kron(across_groups, w_filter[0]), jnp.kron(across_groups, w_gate[0])], axis=1
    )
    return (current_tab, earlier_tab)


def gated_units(cell_input, current_tab, earlier_tab, bias_filter, bias_gate):
    block_rows, block_cols, block_size, features = cell_input.shape
    group_members = 128 // bias_filter.shape[0]
    grouped = cell_input.reshape(block_rows * block_cols * block_size, features // 128, 128)
    shifted = jnp.concatenate([jnp.zeros_like(grouped), grouped[:, :-1]], axis=1)
    pre_both = jnp.einsum("ngk,kj->ngj", grouped, current_tab, preferred_element_type=jnp.float32)
    pre_both = pre_both + jnp.einsum(
        "ngk,kj->ngj", shifted, earlier_tab, preferred_element_type=jnp.float32
    )
    filter_bias = jnp.tile(bias_filter, group_members)
    gate_bias = jnp.tile(bias_gate, group_members)
    gated = jnp.tanh(pre_both[..., :128] + filter_bias) * jax.nn.sigmoid(
        pre_both[..., 128:] + gate_bias
    )
    return gated.astype(jnp.bfloat16).reshape(cell_input.shape)


def shift_pairs(size, step):
    if step > 0:
        return [(i, i + 1) for i in range(size - 1)]
    return [(i + 1, i) for i in range(size - 1)]


def fetch_halo(signal):
    n_rx, n_ry = lax.axis_size("rx"), lax.axis_size("ry")
    above = lax.ppermute(signal[-1:], "rx", shift_pairs(n_rx, 1))
    below = lax.ppermute(signal[:1], "rx", shift_pairs(n_rx, -1))
    left = lax.ppermute(signal[:, -1:], "ry", shift_pairs(n_ry, 1))
    right = lax.ppermute(signal[:, :1], "ry", shift_pairs(n_ry, -1))
    return above, below, left, right


def local_terms(signal, tiles, halo):
    above, below, left, right = halo
    neighbours = (
        signal,
        jnp.concatenate([above, signal[:-1]], axis=0),
        jnp.concatenate([signal[1:], below], axis=0),
        jnp.concatenate([left, signal[:, :-1]], axis=1),
        jnp.concatenate([signal[:, 1:], right], axis=1),
    )
    stencil_sum = jnp.einsum(
        "ijab,ijbf->ijaf", tiles[:, :, 0], neighbours[0], preferred_element_type=jnp.float32
    )
    for offset in range(1, 5):
        stencil_sum = stencil_sum + jnp.einsum(
            "ijab,ijbf->ijaf",
            tiles[:, :, offset],
            neighbours[offset],
            preferred_element_type=jnp.float32,
        )
    return stencil_sum


def edge_select(out_dev, senders):
    destinations = out_dev.reshape(-1)
    owners = jnp.arange(senders, dtype=jnp.int32)
    dest_hits = (destinations[:, None] == owners[None, :]).astype(jnp.int32)
    edge_ranks = jnp.sum((jnp.cumsum(dest_hits, axis=0) - 1) * dest_hits, axis=1)
    slot_ids = jnp.arange(CAP, dtype=jnp.int32)
    select = dest_hits[:, :, None] * (edge_ranks[:, None, None] == slot_ids[None, None, :]).astype(
        jnp.int32
    )
    return select.reshape(select.shape[0], -1).astype(jnp.bfloat16)


def edge_slots(out_dev, senders):
    destinations = out_dev.reshape(-1)
    owners = jnp.arange(senders, dtype=jnp.int32)
    dest_hits = (destinations[:, None] == owners[None, :]).astype(jnp.int32)
    edge_ranks = jnp.sum((jnp.cumsum(dest_hits, axis=0) - 1) * dest_hits, axis=1)
    return destinations * CAP + edge_ranks


def product_kernel(src_ref, slot_ref, sig_ref, tile_ref, out_ref):
    out_ref[...] = jnp.zeros(out_ref.shape, out_ref.dtype)

    def body(edge, carry):
        block = sig_ref[src_ref[edge]]
        product = jnp.dot(tile_ref[edge], block, preferred_element_type=jnp.float32)
        out_ref[slot_ref[edge]] = product.astype(out_ref.dtype)
        return carry

    lax.fori_loop(0, tile_ref.shape[0], body, 0, unroll=True)


def send_products(signal, edge_tiles, sources, slots, select, target_col=None):
    block_rows, block_cols, block_size, features = signal.shape
    nblocks = block_rows * block_cols
    edge_count = edge_tiles.shape[0]
    nslots = lax.axis_size("rx") * CAP
    whole = lambda i, s, t: (0, 0, 0)
    products = pl.pallas_call(
        product_kernel,
        out_shape=jax.ShapeDtypeStruct((nslots, block_size, features), jnp.bfloat16),
        grid_spec=pltpu.PrefetchScalarGridSpec(
            num_scalar_prefetch=2,
            grid=(1,),
            in_specs=[
                pl.BlockSpec((nblocks, block_size, features), whole),
                pl.BlockSpec((edge_count, block_size, block_size), whole),
            ],
            out_specs=pl.BlockSpec((nslots, block_size, features), whole),
        ),
        cost_estimate=pl.CostEstimate(
            flops=2 * edge_count * block_size * block_size * features,
            bytes_accessed=2 * (nblocks + nslots) * block_size * features
            + 2 * edge_count * block_size * block_size,
            transcendentals=0,
        ),
    )(sources, slots, signal.reshape(nblocks, block_size, features), edge_tiles)
    if target_col is None:
        return products.reshape(lax.axis_size("rx"), CAP, block_size, features)
    slot_targets = jnp.einsum(
        "es,ek->sk", select, target_col, preferred_element_type=jnp.float32
    ).astype(jnp.bfloat16)
    payload = jnp.concatenate([products.reshape(nslots, -1), slot_targets], axis=1)
    return payload.reshape(lax.axis_size("rx"), CAP, -1)


def send_products_xla(signal, edge_tiles, sources, select, target_col):
    block_rows, block_cols, block_size, features = signal.shape
    flat = signal.reshape(block_rows * block_cols, block_size, features)
    products = jnp.einsum(
        "eab,ebf->eaf", edge_tiles, flat[sources], preferred_element_type=jnp.float32
    ).astype(jnp.bfloat16)
    products = jnp.concatenate([products.reshape(products.shape[0], -1), target_col], axis=1)
    slots = jnp.einsum(
        "es,ek->sk", select, products, preferred_element_type=jnp.float32
    ).astype(jnp.bfloat16)
    return slots.reshape(lax.axis_size("rx"), CAP, -1)


def far_terms(received, targets, nblocks):
    onehot = (targets[None] == jnp.arange(nblocks, dtype=jnp.int32)[:, None, None]).astype(
        jnp.bfloat16
    )
    received = received.reshape(received.shape[0], received.shape[1], -1)
    return jnp.einsum("nrc,rck->nk", onehot, received, preferred_element_type=jnp.float32)


def local(
    cell_input,
    w_filter,
    w_gate,
    bias_filter,
    bias_gate,
    adjacency,
    out_block,
    out_dev,
    out_target,
    out_tiles,
    w_mix,
    bias_mix,
):
    channels = w_filter.shape[1]
    block_rows, block_cols, block_size, features = cell_input.shape
    nblocks = block_rows * block_cols
    n_rx = lax.axis_size("rx")
    tiles = adjacency.reshape(block_rows, block_cols, 5, block_size, block_size)
    current_tab, earlier_tab = time_tables(w_filter, w_gate, channels)
    gated = gated_units(cell_input, current_tab, earlier_tab, bias_filter, bias_gate)

    select = edge_select(out_dev, n_rx)
    sources = out_block.reshape(-1)
    edge_tiles = out_tiles.reshape(-1, block_size, block_size)
    slots = edge_slots(out_dev, n_rx)
    edge_count = sources.shape[0]
    block_len = block_size * features
    target_col = jnp.zeros((edge_count, 128), jnp.bfloat16).at[:, 0].set(
        (out_target.reshape(-1) + 1).astype(jnp.bfloat16)
    )

    send_one = send_products_xla(gated, edge_tiles, sources, select, target_col)
    halo_one = fetch_halo(gated)
    recv_one = lax.all_to_all(send_one, "rx", split_axis=0, concat_axis=0, tiled=True)
    targets = recv_one[:, :, block_len].astype(jnp.int32) - 1
    near_one = local_terms(gated, tiles, halo_one)
    far_one = far_terms(recv_one, targets, nblocks)[:, :block_len]
    first_hop = (near_one + far_one.reshape(gated.shape)).astype(jnp.bfloat16)

    send_two = send_products(first_hop, edge_tiles, sources, slots, select)
    halo_two = fetch_halo(first_hop)
    recv_two = lax.all_to_all(send_two, "rx", split_axis=0, concat_axis=0, tiled=True)
    near_two = local_terms(first_hop, tiles, halo_two)
    far_two = far_terms(recv_two, targets, nblocks)
    second_hop = near_two + far_two.reshape(gated.shape)

    input_signals, output_signals = group_eye(channels)
    diagonal = (input_signals == output_signals).astype(jnp.float32)
    mix_weights = w_mix.astype(jnp.float32)
    table_zero = jnp.kron(diagonal.astype(jnp.bfloat16), w_mix[0])
    table_one = jnp.kron(diagonal.astype(jnp.bfloat16), w_mix[1])
    table_two = jnp.kron(diagonal, mix_weights[2])
    grouped_shape = (nblocks * block_size, features // 128, 128)
    mixture = jnp.einsum(
        "ngk,kj->ngj", gated.reshape(grouped_shape), table_zero, preferred_element_type=jnp.float32
    )
    mixture = mixture + jnp.einsum(
        "ngk,kj->ngj",
        first_hop.reshape(grouped_shape),
        table_one,
        preferred_element_type=jnp.float32,
    )
    mixture = mixture + jnp.einsum(
        "ngk,kj->ngj", second_hop.reshape(grouped_shape), table_two, precision=lax.Precision.HIGHEST
    )
    mixture = mixture + jnp.tile(bias_mix, 128 // channels)
    output_sum = cell_input.astype(jnp.float32) + mixture.reshape(cell_input.shape)
    return output_sum.astype(jnp.bfloat16)


def solution(mesh):
    in_specs = (
        P("rx", "ry", None, None),
        P(),
        P(),
        P(),
        P(),
        P("rx", "ry", None, None),
        P("rx", "ry", None),
        P("rx", "ry", None, None),
        P("rx", "ry", None),
        P("rx", "ry", None, None),
        P(),
        P(),
    )
    out_specs = P("rx", "ry", None, None)
    return jax.shard_map(local, mesh=mesh, in_specs=in_specs, out_specs=out_specs, check_vma=False)
```

```python
import jax
import jax.numpy as jnp
from jax import lax
from jax.experimental import pallas as pl
from jax.experimental.pallas import tpu as pltpu
from jax.sharding import PartitionSpec as P

DILATION_STEP = 2
CAP = 2


def group_eye(channels):
    group_members = 128 // channels
    input_signals = jnp.arange(group_members, dtype=jnp.int32)[:, None]
    output_signals = jnp.arange(group_members, dtype=jnp.int32)[None, :]
    return (input_signals, output_signals)


def time_tables(w_filter, w_gate, channels):
    group_members = 128 // channels
    input_signals, output_signals = group_eye(channels)
    diagonal = (input_signals == output_signals).astype(jnp.bfloat16)
    within_group = (input_signals == output_signals - DILATION_STEP).astype(jnp.bfloat16)
    across_groups = (input_signals == output_signals - DILATION_STEP + group_members).astype(
        jnp.bfloat16
    )
    current_tab = jnp.concatenate(
        [
            jnp.kron(diagonal, w_filter[1]) + jnp.kron(within_group, w_filter[0]),
            jnp.kron(diagonal, w_gate[1]) + jnp.kron(within_group, w_gate[0]),
        ],
        axis=1,
    )
    earlier_tab = jnp.concatenate(
        [jnp.kron(across_groups, w_filter[0]), jnp.kron(across_groups, w_gate[0])], axis=1
    )
    return (current_tab, earlier_tab)


def gated_units(cell_input, current_tab, earlier_tab, bias_filter, bias_gate):
    block_rows, block_cols, block_size, features = cell_input.shape
    group_members = 128 // bias_filter.shape[0]
    grouped = cell_input.reshape(block_rows * block_cols * block_size, features // 128, 128)
    shifted = jnp.concatenate([jnp.zeros_like(grouped), grouped[:, :-1]], axis=1)
    pre_both = jnp.einsum("ngk,kj->ngj", grouped, current_tab, preferred_element_type=jnp.float32)
    pre_both = pre_both + jnp.einsum(
        "ngk,kj->ngj", shifted, earlier_tab, preferred_element_type=jnp.float32
    )
    filter_bias = jnp.tile(bias_filter, group_members)
    gate_bias = jnp.tile(bias_gate, group_members)
    gated = jnp.tanh(pre_both[..., :128] + filter_bias) * jax.nn.sigmoid(
        pre_both[..., 128:] + gate_bias
    )
    return gated.astype(jnp.bfloat16).reshape(cell_input.shape)


def shift_pairs(size, step):
    if step > 0:
        return [(i, i + 1) for i in range(size - 1)]
    return [(i + 1, i) for i in range(size - 1)]


def fetch_halo(signal):
    n_rx, n_ry = lax.axis_size("rx"), lax.axis_size("ry")
    above = lax.ppermute(signal[-1:], "rx", shift_pairs(n_rx, 1))
    below = lax.ppermute(signal[:1], "rx", shift_pairs(n_rx, -1))
    left = lax.ppermute(signal[:, -1:], "ry", shift_pairs(n_ry, 1))
    right = lax.ppermute(signal[:, :1], "ry", shift_pairs(n_ry, -1))
    return above, below, left, right


def local_terms(signal, tiles, halo):
    above, below, left, right = halo
    neighbours = (
        signal,
        jnp.concatenate([above, signal[:-1]], axis=0),
        jnp.concatenate([signal[1:], below], axis=0),
        jnp.concatenate([left, signal[:, :-1]], axis=1),
        jnp.concatenate([signal[:, 1:], right], axis=1),
    )
    stencil_sum = jnp.einsum(
        "ijab,ijbf->ijaf", tiles[:, :, 0], neighbours[0], preferred_element_type=jnp.float32
    )
    for offset in range(1, 5):
        stencil_sum = stencil_sum + jnp.einsum(
            "ijab,ijbf->ijaf",
            tiles[:, :, offset],
            neighbours[offset],
            preferred_element_type=jnp.float32,
        )
    return stencil_sum


def edge_select(out_dev, senders):
    destinations = out_dev.reshape(-1)
    owners = jnp.arange(senders, dtype=jnp.int32)
    dest_hits = (destinations[:, None] == owners[None, :]).astype(jnp.int32)
    edge_ranks = jnp.sum((jnp.cumsum(dest_hits, axis=0) - 1) * dest_hits, axis=1)
    slot_ids = jnp.arange(CAP, dtype=jnp.int32)
    select = dest_hits[:, :, None] * (edge_ranks[:, None, None] == slot_ids[None, None, :]).astype(
        jnp.int32
    )
    return select.reshape(select.shape[0], -1).astype(jnp.bfloat16)


def edge_slots(out_dev, senders):
    destinations = out_dev.reshape(-1)
    owners = jnp.arange(senders, dtype=jnp.int32)
    dest_hits = (destinations[:, None] == owners[None, :]).astype(jnp.int32)
    edge_ranks = jnp.sum((jnp.cumsum(dest_hits, axis=0) - 1) * dest_hits, axis=1)
    return destinations * CAP + edge_ranks


def product_kernel(src_ref, slot_ref, sig_ref, tile_ref, out_ref):
    out_ref[...] = jnp.zeros(out_ref.shape, out_ref.dtype)

    def body(edge, carry):
        block = sig_ref[src_ref[edge]]
        product = jnp.dot(tile_ref[edge], block, preferred_element_type=jnp.float32)
        out_ref[slot_ref[edge]] = product.astype(out_ref.dtype)
        return carry

    lax.fori_loop(0, tile_ref.shape[0], body, 0, unroll=True)


def send_products(signal, edge_tiles, sources, slots, select, target_col=None):
    block_rows, block_cols, block_size, features = signal.shape
    nblocks = block_rows * block_cols
    edge_count = edge_tiles.shape[0]
    nslots = lax.axis_size("rx") * CAP
    whole = lambda i, s, t: (0, 0, 0)
    products = pl.pallas_call(
        product_kernel,
        out_shape=jax.ShapeDtypeStruct((nslots, block_size, features), jnp.bfloat16),
        grid_spec=pltpu.PrefetchScalarGridSpec(
            num_scalar_prefetch=2,
            grid=(1,),
            in_specs=[
                pl.BlockSpec((nblocks, block_size, features), whole),
                pl.BlockSpec((edge_count, block_size, block_size), whole),
            ],
            out_specs=pl.BlockSpec((nslots, block_size, features), whole),
        ),
        cost_estimate=pl.CostEstimate(
            flops=2 * edge_count * block_size * block_size * features,
            bytes_accessed=2 * (nblocks + nslots) * block_size * features
            + 2 * edge_count * block_size * block_size,
            transcendentals=0,
        ),
    )(sources, slots, signal.reshape(nblocks, block_size, features), edge_tiles)
    if target_col is None:
        return products.reshape(lax.axis_size("rx"), CAP, block_size, features)
    slot_targets = jnp.einsum(
        "es,ek->sk", select, target_col, preferred_element_type=jnp.float32
    ).astype(jnp.bfloat16)
    payload = jnp.concatenate([products.reshape(nslots, -1), slot_targets], axis=1)
    return payload.reshape(lax.axis_size("rx"), CAP, -1)


def send_products_xla(signal, edge_tiles, sources, select, target_col):
    block_rows, block_cols, block_size, features = signal.shape
    flat = signal.reshape(block_rows * block_cols, block_size, features)
    products = jnp.einsum(
        "eab,ebf->eaf", edge_tiles, flat[sources], preferred_element_type=jnp.float32
    ).astype(jnp.bfloat16)
    products = jnp.concatenate([products.reshape(products.shape[0], -1), target_col], axis=1)
    slots = jnp.einsum(
        "es,ek->sk", select, products, preferred_element_type=jnp.float32
    ).astype(jnp.bfloat16)
    return slots.reshape(lax.axis_size("rx"), CAP, -1)


def gather_kernel(tgt_ref, near_ref, recv_ref, out_ref):
    out_ref[...] = near_ref[...]

    def body(slot, carry):
        target = tgt_ref[slot]

        @pl.when(target >= 0)
        def _():
            row = jnp.maximum(target, 0)
            out_ref[row] = out_ref[row] + recv_ref[slot].astype(jnp.float32)

        return carry

    lax.fori_loop(0, recv_ref.shape[0], body, 0, unroll=True)


def add_far(near, received, targets):
    nblocks, block_size, features = near.shape
    nslots = targets.shape[0]
    whole = lambda i, t: (0, 0, 0)
    return pl.pallas_call(
        gather_kernel,
        out_shape=jax.ShapeDtypeStruct(near.shape, jnp.float32),
        grid_spec=pltpu.PrefetchScalarGridSpec(
            num_scalar_prefetch=1,
            grid=(1,),
            in_specs=[
                pl.BlockSpec((nblocks, block_size, features), whole),
                pl.BlockSpec((nslots, block_size, features), whole),
            ],
            out_specs=pl.BlockSpec((nblocks, block_size, features), whole),
        ),
        cost_estimate=pl.CostEstimate(
            flops=nslots * block_size * features,
            bytes_accessed=(8 * nblocks + 2 * nslots) * block_size * features,
            transcendentals=0,
        ),
    )(targets, near, received.reshape(nslots, block_size, features))


def far_terms(received, targets, nblocks):
    onehot = (targets[None] == jnp.arange(nblocks, dtype=jnp.int32)[:, None, None]).astype(
        jnp.bfloat16
    )
    received = received.reshape(received.shape[0], received.shape[1], -1)
    return jnp.einsum("nrc,rck->nk", onehot, received, preferred_element_type=jnp.float32)


def local(
    cell_input,
    w_filter,
    w_gate,
    bias_filter,
    bias_gate,
    adjacency,
    out_block,
    out_dev,
    out_target,
    out_tiles,
    w_mix,
    bias_mix,
):
    channels = w_filter.shape[1]
    block_rows, block_cols, block_size, features = cell_input.shape
    nblocks = block_rows * block_cols
    n_rx = lax.axis_size("rx")
    tiles = adjacency.reshape(block_rows, block_cols, 5, block_size, block_size)
    current_tab, earlier_tab = time_tables(w_filter, w_gate, channels)
    gated = gated_units(cell_input, current_tab, earlier_tab, bias_filter, bias_gate)

    select = edge_select(out_dev, n_rx)
    sources = out_block.reshape(-1)
    edge_tiles = out_tiles.reshape(-1, block_size, block_size)
    slots = edge_slots(out_dev, n_rx)
    edge_count = sources.shape[0]
    block_len = block_size * features
    target_col = jnp.zeros((edge_count, 128), jnp.bfloat16).at[:, 0].set(
        (out_target.reshape(-1) + 1).astype(jnp.bfloat16)
    )

    send_one = send_products_xla(gated, edge_tiles, sources, select, target_col)
    halo_one = fetch_halo(gated)
    recv_one = lax.all_to_all(send_one, "rx", split_axis=0, concat_axis=0, tiled=True)
    targets = recv_one[:, :, block_len].astype(jnp.int32) - 1
    near_one = local_terms(gated, tiles, halo_one)
    far_one = far_terms(recv_one, targets, nblocks)[:, :block_len]
    first_hop = (near_one + far_one.reshape(gated.shape)).astype(jnp.bfloat16)

    send_two = send_products(first_hop, edge_tiles, sources, slots, select)
    halo_two = fetch_halo(first_hop)
    recv_two = lax.all_to_all(send_two, "rx", split_axis=0, concat_axis=0, tiled=True)
    near_two = local_terms(first_hop, tiles, halo_two)
    second_hop = add_far(
        near_two.reshape(nblocks, block_size, features), recv_two, targets.reshape(-1)
    ).reshape(gated.shape)

    input_signals, output_signals = group_eye(channels)
    diagonal = (input_signals == output_signals).astype(jnp.float32)
    mix_weights = w_mix.astype(jnp.float32)
    table_zero = jnp.kron(diagonal.astype(jnp.bfloat16), w_mix[0])
    table_one = jnp.kron(diagonal.astype(jnp.bfloat16), w_mix[1])
    table_two = jnp.kron(diagonal, mix_weights[2])
    grouped_shape = (nblocks * block_size, features // 128, 128)
    mixture = jnp.einsum(
        "ngk,kj->ngj", gated.reshape(grouped_shape), table_zero, preferred_element_type=jnp.float32
    )
    mixture = mixture + jnp.einsum(
        "ngk,kj->ngj",
        first_hop.reshape(grouped_shape),
        table_one,
        preferred_element_type=jnp.float32,
    )
    mixture = mixture + jnp.einsum(
        "ngk,kj->ngj", second_hop.reshape(grouped_shape), table_two, precision=lax.Precision.HIGHEST
    )
    mixture = mixture + jnp.tile(bias_mix, 128 // channels)
    output_sum = cell_input.astype(jnp.float32) + mixture.reshape(cell_input.shape)
    return output_sum.astype(jnp.bfloat16)


def solution(mesh):
    in_specs = (
        P("rx", "ry", None, None),
        P(),
        P(),
        P(),
        P(),
        P("rx", "ry", None, None),
        P("rx", "ry", None),
        P("rx", "ry", None, None),
        P("rx", "ry", None),
        P("rx", "ry", None, None),
        P(),
        P(),
    )
    out_specs = P("rx", "ry", None, None)
    return jax.shard_map(local, mesh=mesh, in_specs=in_specs, out_specs=out_specs, check_vma=False)
```
